256 devices in a mesh: ctx: 32 (over z_hi, x, core), head: 8 (over z_lo, y).
Axes of the slice: x: 4, y: 4, z: 8 (z_hi: 4, z_lo: 2; z = z_hi * 2 + z_lo), core: 2. Of those that a mesh axis runs over, the one named last changes fastest.
Arguments:
- activations: bfloat16 [4096, 8192], P('ctx', 'head'), may hold values from -6 to 6
- query_base: bfloat16 [4096, 8192], P('ctx', 'head'), may hold values from -150 to 150
- key_rows: bfloat16 [4096, 1024], P('ctx', 'head'), may hold values from -4 to 4
- values: bfloat16 [4096, 1024], P('ctx', 'head'), may hold values from -6 to 6
- out_cotangent: bfloat16 [4096, 8192], P('ctx', 'head'), may hold values from -0.3984375 to 0.3984375
- adapter_a: bfloat16 [8192, 16], P('head'), may hold values from -0.0625 to 0.0625
- adapter_b: bfloat16 [16, 8192], P(None, 'head'), may hold values from -1.5 to 1.5
- tangent_a: bfloat16 [8192, 16], P('head'), may hold values from -0.0625 to 0.0625
- tangent_b: bfloat16 [16, 8192], P(None, 'head'), may hold values from -1.5 to 1.5
- segment_ids: int32 [4096], P('ctx'), may hold values from 0 to 7, as said below
- doc_starts: int32 [8], replicated, may hold values from 0 to 4095, as said below
Outputs:
- hvp_a: float32 [8192, 16], P('head')
- hvp_b: float32 [16, 8192], P(None, 'head')
The draws below stay inside these ranges and needn't reach their ends.
Inputs may be any that keep to these rules, and one draw needn't show every extreme that they name: `segment_ids`: segment numbers never fall along the tokens, and every number from 0 to 7 occurs. doc_starts[s] is the first position of segment s; starts rise strictly, doc_starts[0] is 0, every later start is 2560 or more, and the last is 4095.
All inputs are finite; a program needn't handle non-finite values.
Results may differ from the reference program's by a relative error of at most 0.0091.
Values may be sent and summed in bfloat16 or wider, within the bound.
A program may use at most 64 MiB of HBM per device.

```python
import math
import jax
import jax.numpy as jnp
from jax import lax

D = 8192
QUERY_HEADS = 64
KEY_VALUE_HEADS = 8
HEAD_SIZE = 128
ADAPTER_RANK = 16
NDOC = 8
PACK_TOKENS = 4096


def doc_layout(key):
    layout_key = jax.random.fold_in(key, 7)
    tail_len = PACK_TOKENS - 5 * PACK_TOKENS // 8
    chosen = jax.random.permutation(layout_key, tail_len - 1)[:NDOC - 2] + 5 * PACK_TOKENS // 8
    last_start = jnp.full((1,), PACK_TOKENS - 1, jnp.int32)
    starts = jnp.concatenate([jnp.zeros((1,), jnp.int32), jnp.sort(chosen).astype(jnp.int32), last_start])
    positions = jnp.arange(PACK_TOKENS, dtype=jnp.int32)
    segments = jnp.sum((positions[:, None] >= starts[None, 1:]).astype(jnp.int32), axis=1).astype(jnp.int32)
    return (segments, starts)


def draw_segment_ids(key, part):
    return doc_layout(key)[0]


def draw_doc_starts(key, part):
    return doc_layout(key)[1]


def key_layout(key):
    random_base_key = jax.random.fold_in(key, 11)
    unscaled_keys = jnp.clip(jax.random.normal(random_base_key, (PACK_TOKENS, KEY_VALUE_HEADS, HEAD_SIZE), jnp.float32), -4.0, 4.0)
    return unscaled_keys


def draw_key_rows(key, part):
    unscaled_keys = key_layout(key)
    return unscaled_keys.reshape(PACK_TOKENS, KEY_VALUE_HEADS * HEAD_SIZE).astype(jnp.bfloat16)


def draw_query_base(key, part):
    random_base_key = jax.random.fold_in(key, 17)
    base = jnp.clip(jax.random.normal(random_base_key, (PACK_TOKENS, QUERY_HEADS, HEAD_SIZE), jnp.float32), -4.0, 4.0)
    return base.reshape(PACK_TOKENS, QUERY_HEADS * HEAD_SIZE).astype(jnp.bfloat16)


def block_scale(stream_key, shape, shards, low, largest):
    def one(position, parts):
        draws = jax.random.uniform(jax.random.fold_in(jax.random.fold_in(stream_key, 6), position), (parts,), jnp.float32, low / len(shards), largest / len(shards))
        return jnp.repeat(jnp.exp(draws), shape[position] // parts).reshape((-1,) + (1,) * (len(shape) - position - 1))

    level = one(*shards[0])
    for cut in shards[1:]:
        level = level * one(*cut)
    return level


def noise(stream_key, shape, width, reach, cuts=(), kind=jnp.bfloat16):
    gain = block_scale(stream_key, shape, cuts, -0.22, 0.18) if cuts else 1.0
    result = jax.random.normal(stream_key, shape, jnp.float32) * width * gain
    return jnp.minimum(jnp.maximum(result, -reach), reach).astype(kind)


def setup_inputs(seed: int = 0) -> dict:
    seeds = jax.random.split(jax.random.key(seed), 12)
    return {
        "activations": noise(seeds[0], (PACK_TOKENS, D), 1.0, 6.0, ((0, 32), (1, 8))),
        "query_base": draw_query_base(jax.random.fold_in(seeds[11], 71), 0),
        "key_rows": draw_key_rows(jax.random.fold_in(seeds[11], 71), 0),
        "values": noise(seeds[3], (PACK_TOKENS, KEY_VALUE_HEADS * HEAD_SIZE), 1.0, 6.0, ((0, 32), (1, 8))),
        "out_cotangent": noise(seeds[4], (PACK_TOKENS, QUERY_HEADS * HEAD_SIZE), 0.05, 0.3984375, ((0, 32), (1, 8))),
        "adapter_a": noise(seeds[5], (D, ADAPTER_RANK), D ** -0.5, 0.0625, ((0, 8),)),
        "adapter_b": noise(seeds[6], (ADAPTER_RANK, QUERY_HEADS * HEAD_SIZE), ADAPTER_RANK ** -0.5, 1.5, ((1, 8),)),
        "tangent_a": noise(seeds[7], (D, ADAPTER_RANK), D ** -0.5, 0.0625, ((0, 8),)),
        "tangent_b": noise(seeds[8], (ADAPTER_RANK, QUERY_HEADS * HEAD_SIZE), ADAPTER_RANK ** -0.5, 1.5, ((1, 8),)),
        "segment_ids": draw_segment_ids(jax.random.fold_in(seeds[11], 71), 0),
        "doc_starts": draw_doc_starts(jax.random.fold_in(seeds[11], 71), 0),
    }


masked_value = -1e+30

def rounded(array_in):
    return lax.optimization_barrier(array_in.astype(jnp.bfloat16)).astype(jnp.float32)

def visible_mask(positions, row_starts, first_key, key_count):
    key_pos = first_key + jnp.arange(key_count, dtype=jnp.int32)
    return (key_pos[None, :] <= positions[:, None]) & (key_pos[None, :] >= row_starts[:, None])

def block_state(queries, tangents, cotangents, key_blk, value_blk, visible, score_scale):
    highest = lax.Precision.HIGHEST
    scores = jnp.einsum('rgd,kd->rgk', queries, key_blk, precision=highest) * score_scale
    slopes = jnp.einsum('rgd,kd->rgk', tangents, key_blk, precision=highest) * score_scale
    value_dots = jnp.einsum('rgd,kd->rgk', cotangents, value_blk, precision=highest)
    mask_three = visible[:, None, :]
    running_max = lax.optimization_barrier(jnp.max(jnp.where(mask_three, scores, masked_value), axis=2))
    weights = jnp.where(mask_three, jnp.exp(scores - running_max[..., None]), 0.0)
    weighted_dots = weights * value_dots
    weighted_slopes = weights * slopes
    weighted_both = weighted_slopes * value_dots
    weight_sum = lax.optimization_barrier(jnp.sum(weights, axis=2))
    along_sum = lax.optimization_barrier(jnp.sum(weighted_dots, axis=2))
    slope_sum = lax.optimization_barrier(jnp.sum(weighted_slopes, axis=2))
    cross_sum = lax.optimization_barrier(jnp.sum(weighted_both, axis=2))
    stacked = rounded(jnp.stack([weights, weighted_dots, weighted_slopes, weighted_both]))
    key_sums = jnp.einsum('trgk,kd->trgd', stacked, key_blk, precision=highest)
    return (running_max, weight_sum, along_sum, slope_sum, cross_sum, key_sums)

def finish(held, score_scale):
    running_max, weight_sum, along_sum, slope_sum, cross_sum, key_sums = held
    delta = along_sum / weight_sum
    mean_slope = slope_sum / weight_sum
    delta_dot = cross_sum / weight_sum - mean_slope * delta
    factor = score_scale / weight_sum
    grad = (key_sums[1] - delta[..., None] * key_sums[0]) * factor[..., None]
    grad_dot = (key_sums[3] - delta[..., None] * key_sums[2] - mean_slope[..., None] * key_sums[1] + (mean_slope * delta - delta_dot)[..., None] * key_sums[0]) * factor[..., None]
    return (grad, grad_dot)

def reference(activations, query_base, key_rows, values, out_cotangent, adapter_a, adapter_b, tangent_a, tangent_b, segment_ids, doc_starts):
    highest = lax.Precision.HIGHEST
    score_scale = 1.0 / math.sqrt(HEAD_SIZE)
    query_group = QUERY_HEADS // KEY_VALUE_HEADS
    low = jnp.dot(activations, adapter_a, preferred_element_type=jnp.float32)
    low_tangent = jnp.dot(activations, tangent_a, preferred_element_type=jnp.float32)
    b_wide = adapter_b.astype(jnp.float32)
    b_tangent = tangent_b.astype(jnp.float32)
    queries = (query_base.astype(jnp.float32) + jnp.dot(low, b_wide, precision=highest)).astype(jnp.bfloat16)
    query_tangent = (jnp.dot(low_tangent, b_wide, precision=highest) + jnp.dot(low, b_tangent, precision=highest)).astype(jnp.bfloat16)
    queries = lax.optimization_barrier(queries)
    query_tangent = lax.optimization_barrier(query_tangent)
    positions = jnp.arange(PACK_TOKENS, dtype=jnp.int32)
    row_starts = jnp.take(doc_starts, segment_ids).astype(jnp.int32)
    block_len = math.gcd(PACK_TOKENS, 512)
    z_blocks = []
    adapter_b_columns = [jnp.zeros((ADAPTER_RANK, query_group * HEAD_SIZE), jnp.float32) for key_value_head in range(KEY_VALUE_HEADS)]
    for block_number in range(PACK_TOKENS // block_len):
        first_row = block_number * block_len
        last_key = first_row + block_len
        visible = visible_mask(positions[first_row:last_key], row_starts[first_row:last_key], 0, last_key)
        z_block = jnp.zeros((block_len, ADAPTER_RANK), jnp.float32)
        for key_value_head in range(KEY_VALUE_HEADS):
            columns = slice(key_value_head * query_group * HEAD_SIZE, (key_value_head + 1) * query_group * HEAD_SIZE)
            q_three = queries[first_row:last_key, columns].astype(jnp.float32).reshape(block_len, query_group, HEAD_SIZE)
            t_three = query_tangent[first_row:last_key, columns].astype(jnp.float32).reshape(block_len, query_group, HEAD_SIZE)
            g_three = out_cotangent[first_row:last_key, columns].astype(jnp.float32).reshape(block_len, query_group, HEAD_SIZE)
            key_blk = key_rows[:last_key, key_value_head * HEAD_SIZE:(key_value_head + 1) * HEAD_SIZE].astype(jnp.float32)
            value_blk = values[:last_key, key_value_head * HEAD_SIZE:(key_value_head + 1) * HEAD_SIZE].astype(jnp.float32)
            held = block_state(q_three, t_three, g_three, key_blk, value_blk, visible, score_scale)
            grad, grad_dot = finish(held, score_scale)
            grad = grad.reshape(block_len, query_group * HEAD_SIZE)
            grad_dot = grad_dot.reshape(block_len, query_group * HEAD_SIZE)
            z_block = z_block + jnp.dot(grad_dot, b_wide[:, columns].T, precision=highest) + jnp.dot(grad, b_tangent[:, columns].T, precision=highest)
            adapter_b_columns[key_value_head] = adapter_b_columns[key_value_head] + jnp.dot(low_tangent[first_row:last_key].T, grad, precision=highest) + jnp.dot(low[first_row:last_key].T, grad_dot, precision=highest)
        z_blocks.append(z_block)
    z_full = jnp.concatenate(z_blocks, axis=0)
    hvp_a = jnp.dot(activations.astype(jnp.float32).T, z_full, precision=highest)
    hvp_b = jnp.concatenate(adapter_b_columns, axis=1)
    return (hvp_a, hvp_b)
```

```python
import functools, math
import jax, jax.numpy as jnp
from jax import lax
from jax.experimental import pallas as pl
from jax.experimental.pallas import tpu as pltpu

HS = 128
NT = (((1,), (1,)), ((), ()))
TN = (((0,), (0,)), ((), ()))
NN = (((1,), (0,)), ((), ()))
f32, bf16 = jnp.float32, jnp.bfloat16


def mm(a, b, dims=NN):
    return lax.dot_general(a, b, dims, preferred_element_type=f32)


def split2(x):
    hi = x.astype(bf16)
    return hi, (x - hi.astype(f32)).astype(bf16)


def split3(x):
    hi = x.astype(bf16)
    r = x - hi.astype(f32)
    mid = r.astype(bf16)
    return hi, mid, (r - mid.astype(f32)).astype(bf16)


def attend_kernel(kb_len, base_fn, docs, seg_s, seg_v, low_ref, qb_ref, cot_ref, b_ref, tb_ref, k_ref, v_ref,
                  z_ref, bp_ref, s_buf, kt, acc, m_ref, q_s, t_s, g_s):
    rows = qb_ref.shape[0]
    heads = qb_ref.shape[1] // HS
    tile = 2
    lanes = tile * rows
    base = base_fn()
    scale = 1.0 / math.sqrt(HS)
    cexp = scale * math.log2(math.e)
    start_first = docs[seg_s[0]]
    start_last = docs[seg_s[rows - 1]]
    lo = start_first // kb_len
    hi = (base + rows - 1) // kb_len + 1
    seg = seg_v[...]
    starts = jnp.zeros((1, rows), jnp.int32)
    for d in range(docs.shape[0]):
        starts = jnp.where(seg == d, docs[d], starts)
    pos = base + lax.broadcasted_iota(jnp.int32, (1, rows), 1)
    starts2 = jnp.concatenate([starts] * tile, axis=1)
    pos2 = jnp.concatenate([pos] * tile, axis=1)

    low = low_ref[0:16, :]
    lowt = low_ref[16:32, :]
    l3 = split3(low)
    lt3 = split3(lowt)
    b = b_ref[...]
    tb = tb_ref[...]
    q_all = mm(jnp.concatenate(l3, 0), jnp.concatenate([b, b, b], 0), TN) + qb_ref[...].astype(f32)
    t_all = mm(jnp.concatenate(lt3 + l3, 0), jnp.concatenate([b, b, b, tb, tb, tb], 0), TN)
    for h in range(heads):
        cols = slice(h * HS, (h + 1) * HS)
        q_s[h] = q_all[:, cols].astype(bf16)
        t_s[h] = t_all[:, cols].astype(bf16)
        g_s[h] = cot_ref[:, cols]

    def build(kb, c):
        off = pl.multiple_of(kb * kb_len, kb_len)
        kt[0:HS, pl.ds(off, kb_len)] = k_ref[pl.ds(off, kb_len), :].T
        kt[HS:HS + 16, pl.ds(off, kb_len)] = jnp.ones((16, kb_len), bf16)
        return c

    lax.fori_loop(lo, hi, build, 0)
    llt = jnp.concatenate([lt3[0], lt3[0], lt3[1], l3[0], l3[0], l3[1]], axis=1)
    z_ref[...] = jnp.zeros_like(z_ref)

    def one_tile(ti, carry):
        q2 = q_s[pl.ds(ti * tile, tile)].reshape(lanes, HS)
        t2 = t_s[pl.ds(ti * tile, tile)].reshape(lanes, HS)
        g2 = g_s[pl.ds(ti * tile, tile)].reshape(lanes, HS)
        m_ref[...] = jnp.full(m_ref.shape, -1e30, f32)

        def pass1(kb, c):
            off = pl.multiple_of(kb * kb_len, kb_len)
            need = (off < start_last) | (off + kb_len - 1 > base)

            @pl.when(need)
            def _():
                s = mm(k_ref[pl.ds(off, kb_len), :], q2, NT)
                kp = off + lax.broadcasted_iota(jnp.int32, (kb_len, lanes), 0)
                s = jnp.where((kp >= starts2) & (kp <= pos2), s, -1e30)
                s_buf[pl.ds(off, kb_len), :] = s
                m_ref[...] = jnp.maximum(m_ref[...], jnp.max(s.reshape(kb_len // 8, 8, lanes), axis=0))

            @pl.when(jnp.logical_not(need))
            def _():
                s = mm(k_ref[pl.ds(off, kb_len), :], q2, NT)
                s_buf[pl.ds(off, kb_len), :] = s
                m_ref[...] = jnp.maximum(m_ref[...], jnp.max(s.reshape(kb_len // 8, 8, lanes), axis=0))
            return c

        lax.fori_loop(lo, hi, pass1, 0)
        mc = jnp.max(m_ref[...], axis=0, keepdims=True) * cexp
        acc[...] = jnp.zeros_like(acc)

        def pass2(kb, c):
            off = pl.multiple_of(kb * kb_len, kb_len)
            e = jnp.exp2(s_buf[pl.ds(off, kb_len), :] * cexp - mc)
            t = mm(k_ref[pl.ds(off, kb_len), :], t2, NT)
            p = mm(v_ref[pl.ds(off, kb_len), :], g2, NT)
            w1 = e * p
            w2 = e * t
            w3 = w1 * t
            w = jnp.concatenate([e.astype(bf16), w1.astype(bf16), w2.astype(bf16), w3.astype(bf16)], axis=1)
            acc[...] += mm(kt[:, pl.ds(off, kb_len)], w)
            return c

        lax.fori_loop(lo, hi, pass2, 0)
        a = acc[...]
        k0, k1, k2, k3 = (a[0:HS, n * lanes:(n + 1) * lanes] for n in range(4))
        l, aa, bb, cc = (a[HS:HS + 1, n * lanes:(n + 1) * lanes] for n in range(4))
        inv = 1.0 / l
        delta = aa * inv
        mt = bb * inv * scale
        dd = cc * inv * scale - mt * delta
        f = scale * inv
        grad = (k1 - delta * k0) * f
        gdot = (scale * (k3 - delta * k2) - mt * k1 + (mt * delta - dd) * k0) * f
        gh, gl = split2(grad)
        dh, dl = split2(gdot)
        zz = jnp.zeros((16, rows), f32)
        for j in range(tile):
            off = pl.multiple_of((ti * tile + j) * HS, HS)
            bj = b_ref[:, pl.ds(off, HS)]
            tbj = tb_ref[:, pl.ds(off, HS)]
            ln = slice(j * rows, (j + 1) * rows)
            zz += mm(jnp.concatenate([bj, bj, tbj, tbj], 1),
                     jnp.concatenate([dh[:, ln], dl[:, ln], gh[:, ln], gl[:, ln]], 0))
            r = jnp.concatenate([gh[:, ln], gl[:, ln], gh[:, ln], dh[:, ln], dl[:, ln], dh[:, ln]], axis=1)
            bp_ref[:, pl.ds(off, HS)] = mm(llt, r, NT)
        z_ref[...] += zz
        return carry

    lax.fori_loop(0, heads // tile, one_tile, 0)


def attend(docs, seg, low_t, qb, cot, b, tb, k, v, base_fn, kb_len=256):
    rows = qb.shape[0]
    total = k.shape[0]
    sm = pl.BlockSpec(memory_space=pltpu.SMEM)
    vm = pl.BlockSpec(memory_space=pltpu.VMEM)
    return pl.pallas_call(
        functools.partial(attend_kernel, kb_len, base_fn),
        out_shape=(jax.ShapeDtypeStruct((16, rows), f32), jax.ShapeDtypeStruct((16, qb.shape[1]), f32)),
        in_specs=[sm, sm] + [vm] * 8,
        out_specs=(vm, vm),
        scratch_shapes=[
            pltpu.VMEM((total, 2 * rows), f32),
            pltpu.VMEM((HS + 16, total), bf16),
            pltpu.VMEM((HS + 16, 8 * rows), f32),
            pltpu.VMEM((8, 2 * rows), f32),
            pltpu.VMEM((8, rows, HS), bf16),
            pltpu.VMEM((8, rows, HS), bf16),
            pltpu.VMEM((8, rows, HS), bf16),
        ],
        compiler_params=pltpu.CompilerParams(vmem_limit_bytes=40 << 20),
        name="attend",
    )(docs, seg, seg.reshape(1, rows), low_t, qb, cot, b, tb, k, v)


from jax.sharding import PartitionSpec as P

MESH = pl.DeviceIdType.MESH
NX, NC, NZ = 4, 2, 4
GROUP = NX * NC


def place():
    ctx = lax.axis_index("ctx")
    return ctx, ctx // GROUP, (ctx // NC) % NX, ctx % NC


def at(z, x, core):
    return (z % NZ) * GROUP + (x % NX) * NC + core


def greet(ctx_peers, head_peers):
    barrier = pltpu.get_barrier_semaphore()
    for p in ctx_peers:
        pl.semaphore_signal(barrier, inc=1, device_id={"ctx": p}, device_id_type=MESH)
    for p in head_peers:
        pl.semaphore_signal(barrier, inc=1, device_id={"head": p}, device_id_type=MESH)
    return lambda: pl.semaphore_wait(barrier, len(ctx_peers) + len(head_peers))


def gather_kernel(n_head, k_ref, v_ref, x_ref, a_ref, ta_ref, kall, vall, low_ref,
                  parts, mine, rk, rv, rl, ss, sl):
    ctx, z, x, core = place()
    head = lax.axis_index("head")
    rows = k_ref.shape[0]
    heads = [lax.rem(head + d, n_head) for d in range(1, n_head)]
    left, right = at(z, x + 3, core), at(z, x + 1, core)
    down, up = at(z + 3, x, core), at(z + 1, x, core)
    twin = at(z, x, 1 - core)
    ready = greet([left, right, down, up, twin], heads)

    aa = jnp.concatenate([a_ref[...], ta_ref[...]], axis=0)
    part = mm(aa, x_ref[...], NT)
    mine[...] = part
    parts[pl.ds(head, 1)] = part[None]
    own = pl.ds(pl.multiple_of(ctx * rows, rows), rows)
    kall[own, :] = k_ref[...]
    vall[own, :] = v_ref[...]
    ready()

    sends = []

    def cut(ref, j):
        return ref.at[pl.ds(pl.multiple_of(j * rows, rows), rows), :]

    def push(ref, sem, j, to, src=None):
        c = pltpu.make_async_remote_copy(
            src_ref=cut(ref, j) if src is None else src, dst_ref=cut(ref, j), send_sem=ss.at[len(sends)],
            recv_sem=sem.at[j], device_id={"ctx": to}, device_id_type=MESH)
        c.start()
        sends.append(c)

    def push_k(j, to, src=None):
        push(kall, rk, j, to, src)

    def push_v(j, to, src=None):
        push(vall, rv, j, to, src)

    def arrive(ref, sem, j):
        pltpu.make_async_remote_copy(
            src_ref=cut(ref, j), dst_ref=cut(ref, j), send_sem=ss.at[0], recv_sem=sem.at[j],
            device_id={"ctx": twin}, device_id_type=MESH).wait_recv()

    for to in (right, left, up, down, twin):
        push_k(ctx, to, k_ref)
        push_v(ctx, to, v_ref)
    lows = []
    for i, p in enumerate(heads):
        c = pltpu.make_async_remote_copy(
            src_ref=mine, dst_ref=parts.at[head], send_sem=sl.at[i], recv_sem=rl.at[head],
            device_id={"head": p}, device_id_type=MESH)
        c.start()
        lows.append(c)

    def row(zz):
        jl, jr = at(zz, x + 3, core), at(zz, x + 1, core)
        arrive(kall, rk, jl)
        push_k(jl, right)
        arrive(vall, rv, jr)
        push_v(jr, left)
        arrive(vall, rv, jl)
        arrive(kall, rk, jr)
        for j in (jl, jr):
            push_k(j, twin)
            push_v(j, twin)

    def column(j):
        arrive(kall, rk, j)
        for to in (right, left, twin):
            push_k(j, to)
        arrive(vall, rv, j)
        for to in (right, left, twin):
            push_v(j, to)

    jd, ju, jo = at(z + 3, x, core), at(z + 1, x, core), at(z + 2, x, core)
    arrive(kall, rk, jd)
    push_k(jd, up)
    arrive(vall, rv, ju)
    push_v(ju, down)
    for to in (right, left, twin):
        push_k(jd, to)
        push_v(ju, to)
    arrive(vall, rv, jd)
    arrive(kall, rk, ju)
    for to in (right, left, twin):
        push_v(jd, to)
        push_k(ju, to)
    row(z)
    column(jo)
    for i, p in enumerate(heads):
        pltpu.make_async_remote_copy(
            src_ref=mine, dst_ref=parts.at[p], send_sem=sl.at[i], recv_sem=rl.at[p],
            device_id={"head": p}, device_id_type=MESH).wait_recv()
    low_ref[...] = jnp.sum(parts[...], axis=0)
    row(z + 3)
    row(z + 1)
    row(z + 2)
    for d in (0, 3, 1, 2):
        j = at(z + d, x + 2, core)
        arrive(kall, rk, j)
        push_k(j, twin)
        arrive(vall, rv, j)
        push_v(j, twin)
    for zz in range(NZ):
        for xx in range(NX):
            j = at(zz, xx, 1 - core)
            arrive(kall, rk, j)
            arrive(vall, rv, j)
    for c in sends + lows:
        c.wait_send()


def gather(k, v, x, a_t, ta_t, n_ctx, n_head):
    rows, width = k.shape
    vm = pl.BlockSpec(memory_space=pltpu.VMEM)
    return pl.pallas_call(
        functools.partial(gather_kernel, n_head),
        out_shape=(jax.ShapeDtypeStruct((n_ctx * rows, width), bf16), jax.ShapeDtypeStruct((n_ctx * rows, width), bf16),
                   jax.ShapeDtypeStruct((32, rows), f32)),
        in_specs=[vm] * 5,
        out_specs=(vm,) * 3,
        scratch_shapes=[
            pltpu.VMEM((n_head, 32, rows), f32),
            pltpu.VMEM((32, rows), f32),
            pltpu.SemaphoreType.DMA((n_ctx,)),
            pltpu.SemaphoreType.DMA((n_ctx,)),
            pltpu.SemaphoreType.DMA((n_head,)),
            pltpu.SemaphoreType.DMA((64,)),
            pltpu.SemaphoreType.DMA((n_head,)),
        ],
        compiler_params=pltpu.CompilerParams(collective_id=0, has_side_effects=True),
        name="gather",
    )(k, v, x, a_t, ta_t)


def reduce_kernel(n_head, zp_ref, bp_ref, x_ref, oa_ref, ob_ref, zbuf, sa, sb, ra, rb, ca, cb, ta, tb,
                  rz, zs, rsa, rsb, ssa, ssb, rca, rcb, sca, scb, rga, rgb, sga, sgb):
    ctx, z, x, core = place()
    u = lax.rem(ctx, GROUP)
    head = lax.axis_index("head")
    heads = [lax.rem(head + d, n_head) for d in range(1, n_head)]
    mates = [lax.rem(u + d, GROUP) for d in range(1, GROUP)]
    cols = [lax.rem(z + d, NZ) for d in range(1, NZ)]
    ready = greet([z * GROUP + m for m in mates] + [c * GROUP + u for c in cols], heads)
    zbuf[pl.ds(head, 1)] = zp_ref[...][None]
    for i in range(GROUP):
        sb[i] = bp_ref[:, i * HS:(i + 1) * HS]
    ready()
    sends = []

    def copy(src, dst, ssem, rsem, dev):
        return pltpu.make_async_remote_copy(src_ref=src, dst_ref=dst, send_sem=ssem, recv_sem=rsem,
                                            device_id=dev, device_id_type=MESH)

    def start(c):
        c.start()
        sends.append(c)

    for i, p in enumerate(heads):
        start(copy(zp_ref, zbuf.at[head], zs.at[i], rz.at[head], {"head": p}))

    def scatter(s, r, ssem, rsem):
        for i, m in enumerate(mates):
            start(copy(s.at[m], r.at[u], ssem.at[i], rsem.at[u], {"ctx": z * GROUP + m}))
        r[pl.ds(u, 1)] = s[pl.ds(u, 1)]

    def across(r, c, s, rsem, ssem2, rsem2):
        for i, m in enumerate(mates):
            copy(r.at[m], r.at[m], ssem2.at[0], rsem.at[m], {"ctx": z * GROUP + m}).wait_recv()
        part = jnp.sum(r[...], axis=0)
        s[...] = part
        c[pl.ds(z, 1)] = part[None]
        for i, q in enumerate(cols):
            start(copy(s, c.at[z], ssem2.at[i], rsem2.at[z], {"ctx": q * GROUP + u}))

    def spread(c, t, o, ssem, rsem, ssem2, rsem2):
        for i, q in enumerate(cols):
            copy(t.at[q], c.at[q], ssem.at[0], rsem.at[q], {"ctx": q * GROUP + u}).wait_recv()
        t[pl.ds(u, 1)] = jnp.sum(c[...], axis=0)[None]
        for i, m in enumerate(mates):
            start(copy(t.at[u], t.at[u], ssem2.at[i], rsem2.at[u], {"ctx": z * GROUP + m}))

    def collect(t, o, ssem, rsem):
        for m in mates:
            copy(t.at[m], t.at[m], ssem.at[0], rsem.at[m], {"ctx": z * GROUP + m}).wait_recv()
        for i in range(GROUP):
            o[:, i * HS:(i + 1) * HS] = t[i]

    scatter(sb, rb, ssb, rsb)
    for i, p in enumerate(heads):
        copy(zp_ref, zbuf.at[p], zs.at[0], rz.at[p], {"head": p}).wait_recv()
    zsum = jnp.sum(zbuf[...], axis=0)
    ap = mm(jnp.concatenate(split3(zsum), 0), x_ref[...])
    ap = ap[0:16] + ap[16:32] + ap[32:48]
    for i in range(GROUP):
        sa[i] = ap[:, i * HS:(i + 1) * HS]
    scatter(sa, ra, ssa, rsa)
    across(rb, cb, sb_part(sb), rsb, scb, rcb)
    across(ra, ca, sb_part(sa), rsa, sca, rca)
    spread(cb, tb, ob_ref, scb, rcb, sgb, rgb)
    spread(ca, ta, oa_ref, sca, rca, sga, rga)
    collect(tb, ob_ref, sgb, rgb)
    collect(ta, oa_ref, sga, rga)
    for c in sends:
        c.wait_send()


def sb_part(s):
    return s.at[GROUP]


def reduce(zp, bp, x, n_head):
    width = bp.shape[1]
    vm = pl.BlockSpec(memory_space=pltpu.VMEM)
    out = jax.ShapeDtypeStruct((16, width), f32)
    dma = pltpu.SemaphoreType.DMA
    return pl.pallas_call(
        functools.partial(reduce_kernel, n_head),
        out_shape=(out, out),
        in_specs=[vm] * 3,
        out_specs=(vm, vm),
        scratch_shapes=[
            pltpu.VMEM((n_head,) + zp.shape, f32),
            pltpu.VMEM((GROUP + 1, 16, HS), f32), pltpu.VMEM((GROUP + 1, 16, HS), f32),
            pltpu.VMEM((GROUP, 16, HS), f32), pltpu.VMEM((GROUP, 16, HS), f32),
            pltpu.VMEM((NZ, 16, HS), f32), pltpu.VMEM((NZ, 16, HS), f32),
            pltpu.VMEM((GROUP, 16, HS), f32), pltpu.VMEM((GROUP, 16, HS), f32),
            dma((n_head,)), dma((n_head,)),
            dma((GROUP,)), dma((GROUP,)), dma((GROUP,)), dma((GROUP,)),
            dma((NZ,)), dma((NZ,)), dma((NZ,)), dma((NZ,)),
            dma((GROUP,)), dma((GROUP,)), dma((GROUP,)), dma((GROUP,)),
        ],
        compiler_params=pltpu.CompilerParams(collective_id=1, has_side_effects=True),
        name="reduce",
    )(zp, bp, x)


def on_device(n_ctx, n_head, activations, query_base, key_rows, values, out_cotangent, adapter_a, adapter_b, tangent_a, tangent_b,
              segment_ids, doc_starts):
    rows = activations.shape[0]
    kall, vall, low_t = gather(key_rows, values, activations, adapter_a.T, tangent_a.T, n_ctx, n_head)
    zp, bp = attend(doc_starts, segment_ids, low_t, query_base, out_cotangent, adapter_b, tangent_b, kall, vall,
                    base_fn=lambda: lax.axis_index("ctx") * rows, kb_len=KEY_BLOCK)
    oa, ob = reduce(zp, bp, activations, n_head)
    return oa.T, ob


KEY_BLOCK = 1024


def solution(mesh):
    wide = P("ctx", "head")
    placed = (wide,) * 5 + (P("head", None), P(None, "head"), P("head", None), P(None, "head"), P("ctx"), P())
    return jax.shard_map(
        functools.partial(on_device, mesh.shape["ctx"], mesh.shape["head"]),
        mesh=mesh,
        in_specs=placed,
        out_specs=(P("head", None), P(None, "head")),
        check_vma=False,
    )
```

```python
import functools, math
import jax, jax.numpy as jnp
from jax import lax
from jax.experimental import pallas as pl
from jax.experimental.pallas import tpu as pltpu

HS = 128
NT = (((1,), (1,)), ((), ()))
TN = (((0,), (0,)), ((), ()))
NN = (((1,), (0,)), ((), ()))
f32, bf16 = jnp.float32, jnp.bfloat16


def mm(a, b, dims=NN):
    return lax.dot_general(a, b, dims, preferred_element_type=f32)


def split2(x):
    hi = x.astype(bf16)
    return hi, (x - hi.astype(f32)).astype(bf16)


def split3(x):
    hi = x.astype(bf16)
    r = x - hi.astype(f32)
    mid = r.astype(bf16)
    return hi, mid, (r - mid.astype(f32)).astype(bf16)


def attend_kernel(kb_len, base_fn, docs, seg_s, seg_v, low_ref, qb_ref, cot_ref, b_ref, tb_ref, k_ref, v_ref,
                  z_ref, bp_ref, s_buf, kt, acc, m_ref, q_s, t_s, g_s):
    rows = qb_ref.shape[0]
    heads = qb_ref.shape[1] // HS
    tile = 2
    lanes = tile * rows
    base = base_fn()
    scale = 1.0 / math.sqrt(HS)
    cexp = scale * math.log2(math.e)
    start_first = docs[seg_s[0]]
    start_last = docs[seg_s[rows - 1]]
    lo = start_first // kb_len
    hi = (base + rows - 1) // kb_len + 1
    seg = seg_v[...]
    starts = jnp.zeros((1, rows), jnp.int32)
    for d in range(docs.shape[0]):
        starts = jnp.where(seg == d, docs[d], starts)
    pos = base + lax.broadcasted_iota(jnp.int32, (1, rows), 1)
    starts2 = jnp.concatenate([starts] * tile, axis=1)
    pos2 = jnp.concatenate([pos] * tile, axis=1)

    low = low_ref[0:16, :]
    lowt = low_ref[16:32, :]
    l3 = split3(low)
    lt3 = split3(lowt)
    b = b_ref[...]
    tb = tb_ref[...]
    q_all = mm(jnp.concatenate(l3, 0), jnp.concatenate([b, b, b], 0), TN) + qb_ref[...].astype(f32)
    t_all = mm(jnp.concatenate(lt3 + l3, 0), jnp.concatenate([b, b, b, tb, tb, tb], 0), TN)
    for h in range(heads):
        cols = slice(h * HS, (h + 1) * HS)
        q_s[h] = q_all[:, cols].astype(bf16)
        t_s[h] = t_all[:, cols].astype(bf16)
        g_s[h] = cot_ref[:, cols]

    def build(kb, c):
        off = pl.multiple_of(kb * kb_len, kb_len)
        kt[0:HS, pl.ds(off, kb_len)] = k_ref[pl.ds(off, kb_len), :].T
        kt[HS:HS + 16, pl.ds(off, kb_len)] = jnp.ones((16, kb_len), bf16)
        return c

    lax.fori_loop(lo, hi, build, 0)
    llt = jnp.concatenate([lt3[0], lt3[0], lt3[1], l3[0], l3[0], l3[1]], axis=1)
    z_ref[...] = jnp.zeros_like(z_ref)

    def one_tile(ti, carry):
        q2 = q_s[pl.ds(ti * tile, tile)].reshape(lanes, HS)
        t2 = t_s[pl.ds(ti * tile, tile)].reshape(lanes, HS)
        g2 = g_s[pl.ds(ti * tile, tile)].reshape(lanes, HS)
        m_ref[...] = jnp.full(m_ref.shape, -1e30, f32)

        def pass1(kb, c):
            off = pl.multiple_of(kb * kb_len, kb_len)
            need = (off < start_last) | (off + kb_len - 1 > base)

            @pl.when(need)
            def _():
                s = mm(k_ref[pl.ds(off, kb_len), :], q2, NT)
                kp = off + lax.broadcasted_iota(jnp.int32, (kb_len, lanes), 0)
                s = jnp.where((kp >= starts2) & (kp <= pos2), s, -1e30)
                s_buf[pl.ds(off, kb_len), :] = s
                m_ref[...] = jnp.maximum(m_ref[...], jnp.max(s.reshape(kb_len // 8, 8, lanes), axis=0))

            @pl.when(jnp.logical_not(need))
            def _():
                s = mm(k_ref[pl.ds(off, kb_len), :], q2, NT)
                s_buf[pl.ds(off, kb_len), :] = s
                m_ref[...] = jnp.maximum(m_ref[...], jnp.max(s.reshape(kb_len // 8, 8, lanes), axis=0))
            return c

        lax.fori_loop(lo, hi, pass1, 0)
        mc = jnp.max(m_ref[...], axis=0, keepdims=True) * cexp
        acc[...] = jnp.zeros_like(acc)

        def pass2(kb, c):
            off = pl.multiple_of(kb * kb_len, kb_len)
            e = jnp.exp2(s_buf[pl.ds(off, kb_len), :] * cexp - mc)
            t = mm(k_ref[pl.ds(off, kb_len), :], t2, NT)
            p = mm(v_ref[pl.ds(off, kb_len), :], g2, NT)
            w1 = e * p
            w2 = e * t
            w3 = w1 * t
            w = jnp.concatenate([e.astype(bf16), w1.astype(bf16), w2.astype(bf16), w3.astype(bf16)], axis=1)
            acc[...] += mm(kt[:, pl.ds(off, kb_len)], w)
            return c

        lax.fori_loop(lo, hi, pass2, 0)
        a = acc[...]
        k0, k1, k2, k3 = (a[0:HS, n * lanes:(n + 1) * lanes] for n in range(4))
        l, aa, bb, cc = (a[HS:HS + 1, n * lanes:(n + 1) * lanes] for n in range(4))
        inv = 1.0 / l
        delta = aa * inv
        mt = bb * inv * scale
        dd = cc * inv * scale - mt * delta
        f = scale * inv
        grad = (k1 - delta * k0) * f
        gdot = (scale * (k3 - delta * k2) - mt * k1 + (mt * delta - dd) * k0) * f
        gh, gl = split2(grad)
        dh, dl = split2(gdot)
        zz = jnp.zeros((16, rows), f32)
        for j in range(tile):
            off = pl.multiple_of((ti * tile + j) * HS, HS)
            bj = b_ref[:, pl.ds(off, HS)]
            tbj = tb_ref[:, pl.ds(off, HS)]
            ln = slice(j * rows, (j + 1) * rows)
            zz += mm(jnp.concatenate([bj, bj, tbj, tbj], 1),
                     jnp.concatenate([dh[:, ln], dl[:, ln], gh[:, ln], gl[:, ln]], 0))
            r = jnp.concatenate([gh[:, ln], gl[:, ln], gh[:, ln], dh[:, ln], dl[:, ln], dh[:, ln]], axis=1)
            bp_ref[:, pl.ds(off, HS)] = mm(llt, r, NT)
        z_ref[...] += zz
        return carry

    lax.fori_loop(0, heads // tile, one_tile, 0)


def attend(docs, seg, low_t, qb, cot, b, tb, k, v, base_fn, kb_len=256):
    rows = qb.shape[0]
    total = k.shape[0]
    sm = pl.BlockSpec(memory_space=pltpu.SMEM)
    vm = pl.BlockSpec(memory_space=pltpu.VMEM)
    return pl.pallas_call(
        functools.partial(attend_kernel, kb_len, base_fn),
        out_shape=(jax.ShapeDtypeStruct((16, rows), f32), jax.ShapeDtypeStruct((16, qb.shape[1]), f32)),
        in_specs=[sm, sm] + [vm] * 8,
        out_specs=(vm, vm),
        scratch_shapes=[
            pltpu.VMEM((total, 2 * rows), f32),
            pltpu.VMEM((HS + 16, total), bf16),
            pltpu.VMEM((HS + 16, 8 * rows), f32),
            pltpu.VMEM((8, 2 * rows), f32),
            pltpu.VMEM((8, rows, HS), bf16),
            pltpu.VMEM((8, rows, HS), bf16),
            pltpu.VMEM((8, rows, HS), bf16),
        ],
        compiler_params=pltpu.CompilerParams(vmem_limit_bytes=40 << 20),
        name="attend",
    )(docs, seg, seg.reshape(1, rows), low_t, qb, cot, b, tb, k, v)


from jax.sharding import PartitionSpec as P

MESH = pl.DeviceIdType.MESH
NX, NC, NZ = 4, 2, 4
GROUP = NX * NC


def place():
    ctx = lax.axis_index("ctx")
    return ctx, ctx // GROUP, (ctx // NC) % NX, ctx % NC


def at(z, x, core):
    return (z % NZ) * GROUP + (x % NX) * NC + core


def greet(ctx_peers, head_peers):
    barrier = pltpu.get_barrier_semaphore()
    for p in ctx_peers:
        pl.semaphore_signal(barrier, inc=1, device_id={"ctx": p}, device_id_type=MESH)
    for p in head_peers:
        pl.semaphore_signal(barrier, inc=1, device_id={"head": p}, device_id_type=MESH)
    return lambda: pl.semaphore_wait(barrier, len(ctx_peers) + len(head_peers))


def gather_kernel(n_head, k_ref, v_ref, x_ref, a_ref, ta_ref, kall, vall, low_ref,
                  x_s, a_s, parts, mine, rk, rv, rl, ss, sl, loc):
    ctx, z, x, core = place()
    head = lax.axis_index("head")
    rows = k_ref.shape[0]
    heads = [lax.rem(head + d, n_head) for d in range(1, n_head)]
    left, right = at(z, x + 3, core), at(z, x + 1, core)
    down, up = at(z + 3, x, core), at(z + 1, x, core)
    twin = at(z, x, 1 - core)
    ready = greet([left, right, down, up, twin], heads)

    def cut(ref, j):
        return ref.at[pl.ds(pl.multiple_of(j * rows, rows), rows), :]

    loads = [pltpu.make_async_copy(x_ref, x_s, loc.at[0]), pltpu.make_async_copy(a_ref, a_s.at[0:16], loc.at[1]),
             pltpu.make_async_copy(ta_ref, a_s.at[16:32], loc.at[2]),
             pltpu.make_async_copy(k_ref, cut(kall, ctx), loc.at[3]), pltpu.make_async_copy(v_ref, cut(vall, ctx), loc.at[4])]
    for c in loads:
        c.start()
    ready()

    sends = []
    count = [0]

    def push(ref, sem, j, tos, cond=None, src=None):
        for to in tos:
            n = count[0]
            count[0] += 1

            def make(n=n, to=to):
                return pltpu.make_async_remote_copy(
                    src_ref=cut(ref, j) if src is None else src, dst_ref=cut(ref, j), send_sem=ss.at[n],
                    recv_sem=sem.at[j], device_id={"ctx": to}, device_id_type=MESH)

            make().start()
            sends.append((cond, make))

    K, V = (kall, rk), (vall, rv)

    def arrive(kv, j):
        ref, sem = kv
        pltpu.make_async_remote_copy(
            src_ref=cut(ref, j), dst_ref=cut(ref, j), send_sem=ss.at[0], recv_sem=sem.at[j],
            device_id={"ctx": twin}, device_id_type=MESH).wait_recv()

    def when(cond, f):
        if cond is None:
            f()
        else:
            pl.when(cond)(f)

    has = {0: None, 1: z >= 1, 2: z >= 2, 3: z >= 3}
    both, below, first = (z >= 1) & (z <= 2), z <= 2, z == 0
    spot = [[at(z + NZ - d, x + dx, core) for dx in range(NX)] for d in range(NZ)]
    other = [[at(z + NZ - d, xx, 1 - core) for xx in range(NX)] for d in range(NZ)]
    for kv, src in ((K, k_ref), (V, v_ref)):
        when(below, lambda: push(*kv, ctx, [up], below, src))
        when(first, lambda: push(*kv, ctx, [down], first, src))
        push(*kv, ctx, [right, left, twin], None, src)

    loads[0].wait()
    loads[1].wait()
    loads[2].wait()
    part = mm(a_s[...], x_s[...], NT)
    mine[...] = part
    parts[pl.ds(head, 1)] = part[None]
    lows = []
    for i, p in enumerate(heads):
        c = pltpu.make_async_remote_copy(
            src_ref=mine, dst_ref=parts.at[head], send_sem=sl.at[i], recv_sem=rl.at[head],
            device_id={"head": p}, device_id_type=MESH)
        c.start()
        lows.append(c)
    loads[3].wait()
    loads[4].wait()

    def row(d):
        jl, jr = spot[d][3], spot[d][1]
        arrive(K, jl)
        push(*K, jl, [right, twin], has[d])
        arrive(K, jr)
        push(*K, jr, [twin], has[d])
        arrive(V, jr)
        push(*V, jr, [left, twin], has[d])
        arrive(V, jl)
        push(*V, jl, [twin], has[d])

    def column(d):
        j = spot[d][0]
        for kv in (K, V):
            arrive(kv, j)
            if d == 1:
                when(below, lambda: push(*kv, j, [up], both))
            push(*kv, j, [right, left, twin], has[d])

    def far(d):
        j = spot[d][2]
        for kv in (K, V):
            arrive(kv, j)
            push(*kv, j, [twin], has[d])

    def low_sum():
        for i, p in enumerate(heads):
            pltpu.make_async_remote_copy(
                src_ref=mine, dst_ref=parts.at[p], send_sem=sl.at[i], recv_sem=rl.at[p],
                device_id={"head": p}, device_id_type=MESH).wait_recv()
        low_ref[...] = jnp.sum(parts[...], axis=0)

    row(0)
    when(has[1], lambda: column(1))
    when(has[3], lambda: column(3))
    far(0)
    low_sum()
    when(has[1], lambda: row(1))
    when(has[2], lambda: column(2))
    when(has[3], lambda: row(3))
    when(has[1], lambda: far(1))
    when(has[2], lambda: row(2))
    when(has[3], lambda: far(3))
    when(has[2], lambda: far(2))

    def twins(d):
        for xx in range(NX):
            j = other[d][xx]
            arrive(K, j)
            arrive(V, j)

    for d in range(NZ):
        when(has[d], lambda: twins(d))
    groups = {}
    for cond, make in sends:
        groups.setdefault(id(cond), (cond, []))[1].append(make)

    def drain(makes):
        for make in makes:
            make().wait_send()

    for cond, makes in groups.values():
        when(cond, lambda: drain(makes))
    for c in lows:
        c.wait_send()


def gather(k, v, x, a_t, ta_t, n_ctx, n_head):
    rows, width = k.shape
    vm = pl.BlockSpec(memory_space=pltpu.VMEM)
    hb = pl.BlockSpec(memory_space=pltpu.HBM)
    dma = pltpu.SemaphoreType.DMA
    return pl.pallas_call(
        functools.partial(gather_kernel, n_head),
        out_shape=(jax.ShapeDtypeStruct((n_ctx * rows, width), bf16), jax.ShapeDtypeStruct((n_ctx * rows, width), bf16),
                   jax.ShapeDtypeStruct((32, rows), f32)),
        in_specs=[hb] * 5,
        out_specs=(vm,) * 3,
        scratch_shapes=[
            pltpu.VMEM(x.shape, bf16),
            pltpu.VMEM((32, x.shape[1]), bf16),
            pltpu.VMEM((n_head, 32, rows), f32),
            pltpu.VMEM((32, rows), f32),
            dma((n_ctx,)), dma((n_ctx,)), dma((n_head,)), dma((96,)), dma((n_head,)), dma((8,)),
        ],
        compiler_params=pltpu.CompilerParams(collective_id=0, has_side_effects=True, vmem_limit_bytes=8 << 20),
        name="gather",
    )(k, v, x, a_t, ta_t)


def reduce_kernel(n_head, zp_ref, bp_ref, x_ref, oa_ref, ob_ref, zbuf, sa, sb, ra, rb, ca, cb, ta, tb,
                  rz, zs, rsa, rsb, ssa, ssb, rca, rcb, sca, scb, rga, rgb, sga, sgb):
    ctx, z, x, core = place()
    u = lax.rem(ctx, GROUP)
    head = lax.axis_index("head")
    heads = [lax.rem(head + d, n_head) for d in range(1, n_head)]
    mates = [lax.rem(u + d, GROUP) for d in range(1, GROUP)]
    cols = [lax.rem(z + d, NZ) for d in range(1, NZ)]
    ready = greet([z * GROUP + m for m in mates] + [c * GROUP + u for c in cols], heads)
    zbuf[pl.ds(head, 1)] = zp_ref[...][None]
    for i in range(GROUP):
        sb[i] = bp_ref[:, i * HS:(i + 1) * HS]
    ready()
    sends = []

    def copy(src, dst, ssem, rsem, dev):
        return pltpu.make_async_remote_copy(src_ref=src, dst_ref=dst, send_sem=ssem, recv_sem=rsem,
                                            device_id=dev, device_id_type=MESH)

    def start(c):
        c.start()
        sends.append(c)

    for i, p in enumerate(heads):
        start(copy(zp_ref, zbuf.at[head], zs.at[i], rz.at[head], {"head": p}))

    def scatter(s, r, ssem, rsem):
        for i, m in enumerate(mates):
            start(copy(s.at[m], r.at[u], ssem.at[i], rsem.at[u], {"ctx": z * GROUP + m}))
        r[pl.ds(u, 1)] = s[pl.ds(u, 1)]

    def across(r, c, s, rsem, ssem2, rsem2):
        for i, m in enumerate(mates):
            copy(r.at[m], r.at[m], ssem2.at[0], rsem.at[m], {"ctx": z * GROUP + m}).wait_recv()
        part = jnp.sum(r[...], axis=0)
        s[...] = part
        c[pl.ds(z, 1)] = part[None]
        for i, q in enumerate(cols):
            start(copy(s, c.at[z], ssem2.at[i], rsem2.at[z], {"ctx": q * GROUP + u}))

    def spread(c, t, o, ssem, rsem, ssem2, rsem2):
        for i, q in enumerate(cols):
            copy(t.at[q], c.at[q], ssem.at[0], rsem.at[q], {"ctx": q * GROUP + u}).wait_recv()
        t[pl.ds(u, 1)] = jnp.sum(c[...], axis=0)[None]
        for i, m in enumerate(mates):
            start(copy(t.at[u], t.at[u], ssem2.at[i], rsem2.at[u], {"ctx": z * GROUP + m}))

    def collect(t, o, ssem, rsem):
        for m in mates:
            copy(t.at[m], t.at[m], ssem.at[0], rsem.at[m], {"ctx": z * GROUP + m}).wait_recv()
        for i in range(GROUP):
            o[:, i * HS:(i + 1) * HS] = t[i]

    scatter(sb, rb, ssb, rsb)
    for i, p in enumerate(heads):
        copy(zp_ref, zbuf.at[p], zs.at[0], rz.at[p], {"head": p}).wait_recv()
    zsum = jnp.sum(zbuf[...], axis=0)
    ap = mm(jnp.concatenate(split3(zsum), 0), x_ref[...])
    ap = ap[0:16] + ap[16:32] + ap[32:48]
    for i in range(GROUP):
        sa[i] = ap[:, i * HS:(i + 1) * HS]
    scatter(sa, ra, ssa, rsa)
    across(rb, cb, sb_part(sb), rsb, scb, rcb)
    across(ra, ca, sb_part(sa), rsa, sca, rca)
    spread(cb, tb, ob_ref, scb, rcb, sgb, rgb)
    spread(ca, ta, oa_ref, sca, rca, sga, rga)
    collect(tb, ob_ref, sgb, rgb)
    collect(ta, oa_ref, sga, rga)
    for c in sends:
        c.wait_send()


def sb_part(s):
    return s.at[GROUP]


def reduce(zp, bp, x, n_head):
    width = bp.shape[1]
    vm = pl.BlockSpec(memory_space=pltpu.VMEM)
    out = jax.ShapeDtypeStruct((16, width), f32)
    dma = pltpu.SemaphoreType.DMA
    return pl.pallas_call(
        functools.partial(reduce_kernel, n_head),
        out_shape=(out, out),
        in_specs=[vm] * 3,
        out_specs=(vm, vm),
        scratch_shapes=[
            pltpu.VMEM((n_head,) + zp.shape, f32),
            pltpu.VMEM((GROUP + 1, 16, HS), f32), pltpu.VMEM((GROUP + 1, 16, HS), f32),
            pltpu.VMEM((GROUP, 16, HS), f32), pltpu.VMEM((GROUP, 16, HS), f32),
            pltpu.VMEM((NZ, 16, HS), f32), pltpu.VMEM((NZ, 16, HS), f32),
            pltpu.VMEM((GROUP, 16, HS), f32), pltpu.VMEM((GROUP, 16, HS), f32),
            dma((n_head,)), dma((n_head,)),
            dma((GROUP,)), dma((GROUP,)), dma((GROUP,)), dma((GROUP,)),
            dma((NZ,)), dma((NZ,)), dma((NZ,)), dma((NZ,)),
            dma((GROUP,)), dma((GROUP,)), dma((GROUP,)), dma((GROUP,)),
        ],
        compiler_params=pltpu.CompilerParams(collective_id=1, has_side_effects=True, vmem_limit_bytes=4 << 20),
        name="reduce",
    )(zp, bp, x)


def on_device(n_ctx, n_head, activations, query_base, key_rows, values, out_cotangent, adapter_a, adapter_b, tangent_a, tangent_b,
              segment_ids, doc_starts):
    rows = activations.shape[0]
    kall, vall, low_t = gather(key_rows, values, activations, adapter_a.T, tangent_a.T, n_ctx, n_head)
    zp, bp = attend(doc_starts, segment_ids, low_t, query_base, out_cotangent, adapter_b, tangent_b, kall, vall,
                    base_fn=lambda: lax.axis_index("ctx") * rows, kb_len=KEY_BLOCK)
    oa, ob = reduce(zp, bp, activations, n_head)
    return oa.T, ob


KEY_BLOCK = 1024


def solution(mesh):
    wide = P("ctx", "head")
    placed = (wide,) * 5 + (P("head", None), P(None, "head"), P("head", None), P(None, "head"), P("ctx"), P())
    return jax.shard_map(
        functools.partial(on_device, mesh.shape["ctx"], mesh.shape["head"]),
        mesh=mesh,
        in_specs=placed,
        out_specs=(P("head", None), P(None, "head")),
        check_vma=False,
    )
```

```python
import functools, math
import jax, jax.numpy as jnp
from jax import lax
from jax.experimental import pallas as pl
from jax.experimental.pallas import tpu as pltpu

HS = 128
NT = (((1,), (1,)), ((), ()))
TN = (((0,), (0,)), ((), ()))
NN = (((1,), (0,)), ((), ()))
f32, bf16 = jnp.float32, jnp.bfloat16


def mm(a, b, dims=NN):
    return lax.dot_general(a, b, dims, preferred_element_type=f32)


def split2(x):
    hi = x.astype(bf16)
    return hi, (x - hi.astype(f32)).astype(bf16)


def split3(x):
    hi = x.astype(bf16)
    r = x - hi.astype(f32)
    mid = r.astype(bf16)
    return hi, mid, (r - mid.astype(f32)).astype(bf16)


def attend_kernel(kb_len, base_fn, starts_ref, low_ref, qb_ref, cot_ref, b_ref, tb_ref, k_ref, v_ref,
                  z_ref, bp_ref, s_buf, kt, acc, m_ref, q_s, t_s, g_s):
    rows = qb_ref.shape[0]
    heads = qb_ref.shape[1] // HS
    tile = 2
    lanes = tile * rows
    base = base_fn()
    scale = 1.0 / math.sqrt(HS)
    cexp = scale * math.log2(math.e)
    starts = starts_ref[...]
    start_first = jnp.min(starts)
    start_last = jnp.max(starts)
    lo = start_first // kb_len
    hi = (base + rows - 1) // kb_len + 1
    pos = base + lax.broadcasted_iota(jnp.int32, (1, rows), 1)
    starts2 = jnp.concatenate([starts] * tile, axis=1)
    pos2 = jnp.concatenate([pos] * tile, axis=1)

    low = low_ref[0:16, :]
    lowt = low_ref[16:32, :]
    l3 = split3(low)
    lt3 = split3(lowt)
    b = b_ref[...]
    tb = tb_ref[...]
    q_all = mm(jnp.concatenate(l3, 0), jnp.concatenate([b, b, b], 0), TN) + qb_ref[...].astype(f32)
    t_all = mm(jnp.concatenate(lt3 + l3, 0), jnp.concatenate([b, b, b, tb, tb, tb], 0), TN)
    for h in range(heads):
        cols = slice(h * HS, (h + 1) * HS)
        q_s[h] = q_all[:, cols].astype(bf16)
        t_s[h] = t_all[:, cols].astype(bf16)
        g_s[h] = cot_ref[:, cols]

    def build(kb, c):
        off = pl.multiple_of(kb * kb_len, kb_len)
        kt[0:HS, pl.ds(off, kb_len)] = k_ref[pl.ds(off, kb_len), :].T
        kt[HS:HS + 16, pl.ds(off, kb_len)] = jnp.ones((16, kb_len), bf16)
        return c

    lax.fori_loop(lo, hi, build, 0)
    llt = jnp.concatenate([lt3[0], lt3[0], lt3[1], l3[0], l3[0], l3[1]], axis=1)
    z_ref[...] = jnp.zeros_like(z_ref)

    def one_tile(ti, carry):
        q2 = q_s[pl.ds(ti * tile, tile)].reshape(lanes, HS)
        t2 = t_s[pl.ds(ti * tile, tile)].reshape(lanes, HS)
        g2 = g_s[pl.ds(ti * tile, tile)].reshape(lanes, HS)
        m_ref[...] = jnp.full(m_ref.shape, -1e30, f32)

        def pass1(kb, c):
            off = pl.multiple_of(kb * kb_len, kb_len)
            need = (off < start_last) | (off + kb_len - 1 > base)

            @pl.when(need)
            def _():
                s = mm(k_ref[pl.ds(off, kb_len), :], q2, NT)
                kp = off + lax.broadcasted_iota(jnp.int32, (kb_len, lanes), 0)
                s = jnp.where((kp >= starts2) & (kp <= pos2), s, -1e30)
                s_buf[pl.ds(off, kb_len), :] = s
                m_ref[...] = jnp.maximum(m_ref[...], jnp.max(s.reshape(kb_len // 8, 8, lanes), axis=0))

            @pl.when(jnp.logical_not(need))
            def _():
                s = mm(k_ref[pl.ds(off, kb_len), :], q2, NT)
                s_buf[pl.ds(off, kb_len), :] = s
                m_ref[...] = jnp.maximum(m_ref[...], jnp.max(s.reshape(kb_len // 8, 8, lanes), axis=0))
            return c

        lax.fori_loop(lo, hi, pass1, 0)
        mc = jnp.max(m_ref[...], axis=0, keepdims=True) * cexp
        acc[...] = jnp.zeros_like(acc)

        def pass2(kb, c):
            off = pl.multiple_of(kb * kb_len, kb_len)
            e = jnp.exp2(s_buf[pl.ds(off, kb_len), :] * cexp - mc)
            t = mm(k_ref[pl.ds(off, kb_len), :], t2, NT)
            p = mm(v_ref[pl.ds(off, kb_len), :], g2, NT)
            w1 = e * p
            w2 = e * t
            w3 = w1 * t
            w = jnp.concatenate([e.astype(bf16), w1.astype(bf16), w2.astype(bf16), w3.astype(bf16)], axis=1)
            acc[...] += mm(kt[:, pl.ds(off, kb_len)], w)
            return c

        lax.fori_loop(lo, hi, pass2, 0)
        a = acc[...]
        k0, k1, k2, k3 = (a[0:HS, n * lanes:(n + 1) * lanes] for n in range(4))
        l, aa, bb, cc = (a[HS:HS + 1, n * lanes:(n + 1) * lanes] for n in range(4))
        inv = 1.0 / l
        delta = aa * inv
        mt = bb * inv * scale
        dd = cc * inv * scale - mt * delta
        f = scale * inv
        grad = (k1 - delta * k0) * f
        gdot = (scale * (k3 - delta * k2) - mt * k1 + (mt * delta - dd) * k0) * f
        gh, gl = split2(grad)
        dh, dl = split2(gdot)
        zz = jnp.zeros((16, rows), f32)
        for j in range(tile):
            off = pl.multiple_of((ti * tile + j) * HS, HS)
            bj = b_ref[:, pl.ds(off, HS)]
            tbj = tb_ref[:, pl.ds(off, HS)]
            ln = slice(j * rows, (j + 1) * rows)
            zz += mm(jnp.concatenate([bj, bj, tbj, tbj], 1),
                     jnp.concatenate([dh[:, ln], dl[:, ln], gh[:, ln], gl[:, ln]], 0))
            r = jnp.concatenate([gh[:, ln], gl[:, ln], gh[:, ln], dh[:, ln], dl[:, ln], dh[:, ln]], axis=1)
            bp_ref[:, pl.ds(off, HS)] = mm(llt, r, NT)
        z_ref[...] += zz
        return carry

    lax.fori_loop(0, heads // tile, one_tile, 0)


def attend(starts, low_t, qb, cot, b, tb, k, v, base_fn, kb_len=256):
    rows = qb.shape[0]
    total = k.shape[0]
    vm = pl.BlockSpec(memory_space=pltpu.VMEM)
    return pl.pallas_call(
        functools.partial(attend_kernel, kb_len, base_fn),
        out_shape=(jax.ShapeDtypeStruct((16, rows), f32), jax.ShapeDtypeStruct((16, qb.shape[1]), f32)),
        in_specs=[vm] * 8,
        out_specs=(vm, vm),
        scratch_shapes=[
            pltpu.VMEM((total, 2 * rows), f32),
            pltpu.VMEM((HS + 16, total), bf16),
            pltpu.VMEM((HS + 16, 8 * rows), f32),
            pltpu.VMEM((8, 2 * rows), f32),
            pltpu.VMEM((8, rows, HS), bf16),
            pltpu.VMEM((8, rows, HS), bf16),
            pltpu.VMEM((8, rows, HS), bf16),
        ],
        compiler_params=pltpu.CompilerParams(vmem_limit_bytes=40 << 20),
        name="attend",
    )(starts, low_t, qb, cot, b, tb, k, v)


from jax.sharding import PartitionSpec as P

MESH = pl.DeviceIdType.MESH
NX, NC, NZ = 4, 2, 4
GROUP = NX * NC


def place():
    ctx = lax.axis_index("ctx")
    return ctx, ctx // GROUP, (ctx // NC) % NX, ctx % NC


def at(z, x, core):
    return (z % NZ) * GROUP + (x % NX) * NC + core


def greet(ctx_peers, head_peers):
    barrier = pltpu.get_barrier_semaphore()
    for p in ctx_peers:
        pl.semaphore_signal(barrier, inc=1, device_id={"ctx": p}, device_id_type=MESH)
    for p in head_peers:
        pl.semaphore_signal(barrier, inc=1, device_id={"head": p}, device_id_type=MESH)
    return lambda: pl.semaphore_wait(barrier, len(ctx_peers) + len(head_peers))


def gather_kernel(n_head, k_ref, v_ref, x_ref, a_ref, ta_ref, qb_ref, cot_ref, b_ref, tb_ref, seg_ref, docs_ref,
                  kall, vall, low_ref, x_o, qb_o, cot_o, b_o, tb_o, starts_ref,
                  a_s, parts, mine, seg_s, docs_s, rk, rv, rl, ss, sl, loc):
    ctx, z, x, core = place()
    head = lax.axis_index("head")
    rows = k_ref.shape[0]
    heads = [lax.rem(head + d, n_head) for d in range(1, n_head)]
    twin = at(z, x, 1 - core)
    sides = [at(z, x + dx, core) for dx in (1, 3, 2)]
    ahead = [at(z + dz, x, core) for dz in range(NZ)]
    ready = greet(sides + ahead[1:] + [twin], heads)

    def cut(ref, j):
        return ref.at[pl.ds(pl.multiple_of(j * rows, rows), rows), :]

    pairs = [(x_ref, x_o), (a_ref, a_s.at[0:16]), (ta_ref, a_s.at[16:32]), (k_ref, cut(kall, ctx)), (v_ref, cut(vall, ctx)),
             (seg_ref, seg_s), (docs_ref, docs_s), (qb_ref, qb_o), (cot_ref, cot_o), (b_ref, b_o), (tb_ref, tb_o)]
    loads = [pltpu.make_async_copy(s, d, loc.at[i]) for i, (s, d) in enumerate(pairs)]
    for c in loads:
        c.start()
    ready()

    sends = []
    count = [0]

    def push(kv, j, tos, cond=None, src=None):
        ref, sem = kv
        for to in tos:
            n = count[0]
            count[0] += 1

            def make(n=n, to=to):
                return pltpu.make_async_remote_copy(
                    src_ref=cut(ref, j) if src is None else src, dst_ref=cut(ref, j), send_sem=ss.at[n],
                    recv_sem=sem.at[j], device_id={"ctx": to}, device_id_type=MESH)

            make().start()
            sends.append((cond, make))

    K, V = (kall, rk), (vall, rv)

    def arrive(kv, j):
        ref, sem = kv
        pltpu.make_async_remote_copy(
            src_ref=cut(ref, j), dst_ref=cut(ref, j), send_sem=ss.at[0], recv_sem=sem.at[j],
            device_id={"ctx": twin}, device_id_type=MESH).wait_recv()

    def when(cond, f):
        if cond is None:
            f()
        else:
            pl.when(cond)(f)

    has = {0: None, 1: z >= 1, 2: z >= 2, 3: z >= 3}
    to1, to2, to3 = z <= 2, z <= 1, z == 0
    spot = [[at(z + NZ - d, x + dx, core) for dx in range(NX)] for d in range(NZ)]
    other = [[at(z + NZ - d, xx, 1 - core) for xx in range(NX)] for d in range(NZ)]

    for kv, src in ((K, k_ref), (V, v_ref)):
        when(to2, lambda: push(kv, ctx, [ahead[2]], to2, src))
        when(to1, lambda: push(kv, ctx, [ahead[1]], to1, src))
        push(kv, ctx, sides + [twin], None, src)
    for kv, src in ((K, k_ref), (V, v_ref)):
        when(to3, lambda: push(kv, ctx, [ahead[3]], to3, src))

    for c in loads[:3]:
        c.wait()
    part = mm(a_s[...], x_o[...], NT)
    mine[...] = part
    parts[pl.ds(head, 1)] = part[None]
    lows = []
    for i, p in enumerate(heads):
        c = pltpu.make_async_remote_copy(
            src_ref=mine, dst_ref=parts.at[head], send_sem=sl.at[i], recv_sem=rl.at[head],
            device_id={"head": p}, device_id_type=MESH)
        c.start()
        lows.append(c)
    for c in loads[3:]:
        c.wait()
    seg = seg_s[...]
    starts = jnp.zeros(seg.shape, jnp.int32)
    for d in range(docs_s.shape[0]):
        starts = jnp.where(seg == d, docs_s[d], starts)
    starts_ref[...] = starts

    def row(d):
        for kv in (K, V):
            for dx in (1, 3, 2):
                arrive(kv, spot[d][dx])
                push(kv, spot[d][dx], [twin], has[d])

    def column(d):
        for kv in (K, V):
            arrive(kv, spot[d][0])
            push(kv, spot[d][0], sides + [twin], has[d])

    def low_sum():
        for i, p in enumerate(heads):
            pltpu.make_async_remote_copy(
                src_ref=mine, dst_ref=parts.at[p], send_sem=sl.at[i], recv_sem=rl.at[p],
                device_id={"head": p}, device_id_type=MESH).wait_recv()
        low_ref[...] = jnp.sum(parts[...], axis=0)

    when(has[1], lambda: column(1))
    row(0)
    when(has[2], lambda: column(2))
    when(has[3], lambda: column(3))
    low_sum()
    for d in (1, 2, 3):
        when(has[d], lambda: row(d))

    def twins(d):
        for xx in range(NX):
            j = other[d][xx]
            arrive(K, j)
            arrive(V, j)

    for d in range(NZ):
        when(has[d], lambda: twins(d))
    groups = {}
    for cond, make in sends:
        groups.setdefault(id(cond), (cond, []))[1].append(make)

    def drain(makes):
        for make in makes:
            make().wait_send()

    for cond, makes in groups.values():
        when(cond, lambda: drain(makes))
    for c in lows:
        c.wait_send()


def gather(k, v, x, a_t, ta_t, qb, cot, b, tb, seg, docs, n_ctx, n_head):
    rows, width = k.shape
    vm = pl.BlockSpec(memory_space=pltpu.VMEM)
    hb = pl.BlockSpec(memory_space=pltpu.HBM)
    dma = pltpu.SemaphoreType.DMA
    like = jax.ShapeDtypeStruct
    args = (k, v, x, a_t, ta_t, qb, cot, b, tb, seg.reshape(1, rows), docs)
    return pl.pallas_call(
        functools.partial(gather_kernel, n_head),
        out_shape=(like((n_ctx * rows, width), bf16), like((n_ctx * rows, width), bf16), like((32, rows), f32),
                   like(x.shape, bf16), like(qb.shape, bf16), like(cot.shape, bf16), like(b.shape, bf16), like(tb.shape, bf16),
                   like((1, rows), jnp.int32)),
        in_specs=[hb] * 11,
        out_specs=(vm,) * 9,
        scratch_shapes=[
            pltpu.VMEM((32, x.shape[1]), bf16),
            pltpu.VMEM((n_head, 32, rows), f32),
            pltpu.VMEM((32, rows), f32),
            pltpu.VMEM((1, rows), jnp.int32),
            pltpu.SMEM(docs.shape, jnp.int32),
            dma((n_ctx,)), dma((n_ctx,)), dma((n_head,)), dma((96,)), dma((n_head,)), dma((11,)),
        ],
        compiler_params=pltpu.CompilerParams(collective_id=0, has_side_effects=True, vmem_limit_bytes=8 << 20),
        name="gather",
    )(*(pltpu.with_memory_space_constraint(r, pltpu.HBM) for r in args))


def reduce_kernel(n_head, zp_ref, bp_ref, x_ref, oa_ref, ob_ref, zbuf, sa, sb, ra, rb, ca, cb, ta, tb,
                  rz, zs, rsa, rsb, ssa, ssb, rca, rcb, sca, scb, rga, rgb, sga, sgb):
    ctx, z, x, core = place()
    u = lax.rem(ctx, GROUP)
    head = lax.axis_index("head")
    heads = [lax.rem(head + d, n_head) for d in range(1, n_head)]
    mates = [lax.rem(u + d, GROUP) for d in range(1, GROUP)]
    cols = [lax.rem(z + d, NZ) for d in range(1, NZ)]
    ready = greet([z * GROUP + m for m in mates] + [c * GROUP + u for c in cols], heads)
    zbuf[pl.ds(head, 1)] = zp_ref[...][None]
    for i in range(GROUP):
        sb[i] = bp_ref[:, i * HS:(i + 1) * HS]
    ready()
    sends = []

    def copy(src, dst, ssem, rsem, dev):
        return pltpu.make_async_remote_copy(src_ref=src, dst_ref=dst, send_sem=ssem, recv_sem=rsem,
                                            device_id=dev, device_id_type=MESH)

    def start(c):
        c.start()
        sends.append(c)

    for i, p in enumerate(heads):
        start(copy(zp_ref, zbuf.at[head], zs.at[i], rz.at[head], {"head": p}))

    def scatter(s, r, ssem, rsem):
        for i, m in enumerate(mates):
            start(copy(s.at[m], r.at[u], ssem.at[i], rsem.at[u], {"ctx": z * GROUP + m}))
        r[pl.ds(u, 1)] = s[pl.ds(u, 1)]

    def across(r, c, s, rsem, ssem2, rsem2):
        for i, m in enumerate(mates):
            copy(r.at[m], r.at[m], ssem2.at[0], rsem.at[m], {"ctx": z * GROUP + m}).wait_recv()
        part = jnp.sum(r[...], axis=0)
        s[...] = part
        c[pl.ds(z, 1)] = part[None]
        for i, q in enumerate(cols):
            start(copy(s, c.at[z], ssem2.at[i], rsem2.at[z], {"ctx": q * GROUP + u}))

    def spread(c, t, o, ssem, rsem, ssem2, rsem2):
        for i, q in enumerate(cols):
            copy(t.at[q], c.at[q], ssem.at[0], rsem.at[q], {"ctx": q * GROUP + u}).wait_recv()
        t[pl.ds(u, 1)] = jnp.sum(c[...], axis=0)[None]
        for i, m in enumerate(mates):
            start(copy(t.at[u], t.at[u], ssem2.at[i], rsem2.at[u], {"ctx": z * GROUP + m}))

    def collect(t, o, ssem, rsem):
        for m in mates:
            copy(t.at[m], t.at[m], ssem.at[0], rsem.at[m], {"ctx": z * GROUP + m}).wait_recv()
        for i in range(GROUP):
            o[:, i * HS:(i + 1) * HS] = t[i]

    scatter(sb, rb, ssb, rsb)
    for i, p in enumerate(heads):
        copy(zp_ref, zbuf.at[p], zs.at[0], rz.at[p], {"head": p}).wait_recv()
    zsum = jnp.sum(zbuf[...], axis=0)
    ap = mm(jnp.concatenate(split3(zsum), 0), x_ref[...])
    ap = ap[0:16] + ap[16:32] + ap[32:48]
    for i in range(GROUP):
        sa[i] = ap[:, i * HS:(i + 1) * HS]
    scatter(sa, ra, ssa, rsa)
    across(rb, cb, sb_part(sb), rsb, scb, rcb)
    across(ra, ca, sb_part(sa), rsa, sca, rca)
    spread(cb, tb, ob_ref, scb, rcb, sgb, rgb)
    spread(ca, ta, oa_ref, sca, rca, sga, rga)
    collect(tb, ob_ref, sgb, rgb)
    collect(ta, oa_ref, sga, rga)
    for c in sends:
        c.wait_send()


def sb_part(s):
    return s.at[GROUP]


def reduce(zp, bp, x, n_head):
    width = bp.shape[1]
    vm = pl.BlockSpec(memory_space=pltpu.VMEM)
    out = jax.ShapeDtypeStruct((16, width), f32)
    dma = pltpu.SemaphoreType.DMA
    return pl.pallas_call(
        functools.partial(reduce_kernel, n_head),
        out_shape=(out, out),
        in_specs=[vm] * 3,
        out_specs=(vm, vm),
        scratch_shapes=[
            pltpu.VMEM((n_head,) + zp.shape, f32),
            pltpu.VMEM((GROUP + 1, 16, HS), f32), pltpu.VMEM((GROUP + 1, 16, HS), f32),
            pltpu.VMEM((GROUP, 16, HS), f32), pltpu.VMEM((GROUP, 16, HS), f32),
            pltpu.VMEM((NZ, 16, HS), f32), pltpu.VMEM((NZ, 16, HS), f32),
            pltpu.VMEM((GROUP, 16, HS), f32), pltpu.VMEM((GROUP, 16, HS), f32),
            dma((n_head,)), dma((n_head,)),
            dma((GROUP,)), dma((GROUP,)), dma((GROUP,)), dma((GROUP,)),
            dma((NZ,)), dma((NZ,)), dma((NZ,)), dma((NZ,)),
            dma((GROUP,)), dma((GROUP,)), dma((GROUP,)), dma((GROUP,)),
        ],
        compiler_params=pltpu.CompilerParams(collective_id=1, has_side_effects=True, vmem_limit_bytes=4 << 20),
        name="reduce",
    )(zp, bp, x)


def finish_kernel(a_ref, b_ref, oa_ref, ob_ref, sem):
    copies = [pltpu.make_async_copy(a_ref, oa_ref, sem.at[0]), pltpu.make_async_copy(b_ref, ob_ref, sem.at[1])]
    for c in copies:
        c.start()
    for c in copies:
        c.wait()


def finish(a, b):
    vm = pl.BlockSpec(memory_space=pltpu.VMEM)
    hb = pl.BlockSpec(memory_space=pltpu.HBM)
    return pl.pallas_call(
        finish_kernel,
        out_shape=(jax.ShapeDtypeStruct(a.shape, f32), jax.ShapeDtypeStruct(b.shape, f32)),
        in_specs=[vm, vm],
        out_specs=(hb, hb),
        scratch_shapes=[pltpu.SemaphoreType.DMA((2,))],
        compiler_params=pltpu.CompilerParams(vmem_limit_bytes=1 << 20),
        name="finish",
    )(a, b)


def on_device(n_ctx, n_head, activations, query_base, key_rows, values, out_cotangent, adapter_a, adapter_b, tangent_a, tangent_b,
              segment_ids, doc_starts):
    rows = activations.shape[0]
    kall, vall, low_t, x, qb, cot, b, tb, starts = gather(
        key_rows, values, activations, adapter_a.T, tangent_a.T, query_base, out_cotangent, adapter_b, tangent_b,
        segment_ids, doc_starts, n_ctx, n_head)
    zp, bp = attend(starts, low_t, qb, cot, b, tb, kall, vall,
                    base_fn=lambda: lax.axis_index("ctx") * rows, kb_len=KEY_BLOCK)
    oa, ob = finish(*reduce(zp, bp, x, n_head))
    return oa.T, ob


KEY_BLOCK = 1024


def solution(mesh):
    wide = P("ctx", "head")
    placed = (wide,) * 5 + (P("head", None), P(None, "head"), P("head", None), P(None, "head"), P("ctx"), P())
    return jax.shard_map(
        functools.partial(on_device, mesh.shape["ctx"], mesh.shape["head"]),
        mesh=mesh,
        in_specs=placed,
        out_specs=(P("head", None), P(None, "head")),
        check_vma=False,
    )
```

```python
import functools, math
import jax, jax.numpy as jnp
from jax import lax
from jax.experimental import pallas as pl
from jax.experimental.pallas import tpu as pltpu

HS = 128
TILE = 2
ONES = 16
NT = (((1,), (1,)), ((), ()))
TN = (((0,), (0,)), ((), ()))
NN = (((1,), (0,)), ((), ()))
f32, bf16 = jnp.float32, jnp.bfloat16
SCALE = 1.0 / math.sqrt(HS)
CEXP = SCALE * math.log2(math.e)


def mm(a, b, dims=NN):
    return lax.dot_general(a, b, dims, preferred_element_type=f32)


def split2(x):
    hi = x.astype(bf16)
    return hi, (x - hi.astype(f32)).astype(bf16)


def split3(x):
    hi = x.astype(bf16)
    r = x - hi.astype(f32)
    mid = r.astype(bf16)
    return hi, mid, (r - mid.astype(f32)).astype(bf16)


def make_queries(low_t, qb_ref, cot_ref, b, tb, q_s, t_s, g_s):
    l3 = split3(low_t[0:16, :])
    lt3 = split3(low_t[16:32, :])
    q_all = mm(jnp.concatenate(l3, 0), jnp.concatenate([b, b, b], 0), TN) + qb_ref[...].astype(f32)
    t_all = mm(jnp.concatenate(lt3 + l3, 0), jnp.concatenate([b, b, b, tb, tb, tb], 0), TN)
    for h in range(q_s.shape[0]):
        cols = slice(h * HS, (h + 1) * HS)
        q_s[h] = q_all[:, cols].astype(bf16)
        t_s[h] = t_all[:, cols].astype(bf16)
        g_s[h] = cot_ref[:, cols]


def pick(ref, ti):
    v = ref[pl.ds(ti * TILE, TILE)]
    return v.reshape(TILE * v.shape[1], HS)


def weights(s, mc, kblk, vblk, t2, g2):
    e = jnp.exp2(s * CEXP - mc)
    t = mm(kblk, t2, NT)
    p = mm(vblk, g2, NT)
    w1 = e * p
    w2 = e * t
    w3 = w1 * t
    return jnp.concatenate([e.astype(bf16), w1.astype(bf16), w2.astype(bf16), w3.astype(bf16)], axis=1)


def transpose_keys(kblk):
    return jnp.concatenate([kblk.T, jnp.ones((ONES, kblk.shape[0]), bf16)], axis=0)


def own_tile(ti, first, base, starts, kblk, vblk, kt, q_s, t_s, g_s, s_own, acc_o, m_o):
    rows = starts.shape[1]
    n_keys = kblk.shape[0]
    pos = base + lax.broadcasted_iota(jnp.int32, (1, rows), 1)
    starts2 = jnp.concatenate([starts] * TILE, axis=1)
    pos2 = jnp.concatenate([pos] * TILE, axis=1)
    s = mm(kblk[...], pick(q_s, ti), NT)
    kp = first + lax.broadcasted_iota(jnp.int32, s.shape, 0)
    s = jnp.where((kp >= starts2) & (kp <= pos2), s, -1e30)
    s_own[...] = s
    m = jnp.max(jnp.max(s.reshape(n_keys // 8, 8, s.shape[1]), axis=0), axis=0, keepdims=True)
    m_o[ti] = jnp.broadcast_to(m, m_o.shape[1:])
    w = weights(s_own[...], m * CEXP, kblk[...], vblk[...], pick(t_s, ti), pick(g_s, ti))
    acc_o[ti] = mm(kt[...], w)


def attend_kernel(kb_len, own_fn, starts_ref, m_ref, q_s, t_s, g_s, k_ref, v_ref, acc_in, acc, s_buf, kt, m_new):
    lanes = TILE * starts_ref.shape[1]
    starts = starts_ref[...]
    start_last = jnp.max(starts)
    lo = jnp.min(starts) // kb_len
    hi = own_fn()
    starts2 = jnp.concatenate([starts] * TILE, axis=1)

    def build(kb, c):
        off = pl.multiple_of(kb * kb_len, kb_len)
        kt[:, pl.ds(off, kb_len)] = transpose_keys(k_ref[pl.ds(off, kb_len), :])
        return c

    lax.fori_loop(lo, hi, build, 0)

    def one_tile(ti, carry):
        q2, t2, g2 = pick(q_s, ti), pick(t_s, ti), pick(g_s, ti)
        m_old = m_ref[ti]
        m_new[...] = m_old

        def pass1(kb, c):
            off = pl.multiple_of(kb * kb_len, kb_len)

            def keep(s):
                s_buf[pl.ds(off, kb_len), :] = s
                m_new[...] = jnp.maximum(m_new[...], jnp.max(s.reshape(kb_len // 8, 8, lanes), axis=0))

            @pl.when(off < start_last)
            def _():
                s = mm(k_ref[pl.ds(off, kb_len), :], q2, NT)
                kp = off + lax.broadcasted_iota(jnp.int32, (kb_len, lanes), 0)
                keep(jnp.where(kp >= starts2, s, -1e30))

            @pl.when(off >= start_last)
            def _():
                keep(mm(k_ref[pl.ds(off, kb_len), :], q2, NT))
            return c

        lax.fori_loop(lo, hi, pass1, 0)
        m = jnp.max(m_new[...], axis=0, keepdims=True)
        mc = m * CEXP
        factor = jnp.exp2(m_old[0:1] * CEXP - mc)
        acc[ti] = acc[ti] * jnp.concatenate([factor] * 4, axis=1)

        def pass2(kb, c):
            off = pl.multiple_of(kb * kb_len, kb_len)
            w = weights(s_buf[pl.ds(off, kb_len), :], mc, k_ref[pl.ds(off, kb_len), :], v_ref[pl.ds(off, kb_len), :], t2, g2)
            acc[ti] += mm(kt[:, pl.ds(off, kb_len)], w)
            return c

        lax.fori_loop(lo, hi, pass2, 0)
        return carry

    lax.fori_loop(0, jnp.where(lo < hi, acc.shape[0], 0), one_tile, 0)


def attend(starts, m_o, q_s, t_s, g_s, k, v, acc, own_fn, kb_len):
    total = k.shape[0]
    lanes = TILE * starts.shape[1]
    vm = pl.BlockSpec(memory_space=pltpu.VMEM)
    return pl.pallas_call(
        functools.partial(attend_kernel, kb_len, own_fn),
        out_shape=jax.ShapeDtypeStruct(acc.shape, f32),
        in_specs=[vm] * 8,
        out_specs=vm,
        scratch_shapes=[
            pltpu.VMEM((total, lanes), f32),
            pltpu.VMEM((HS + ONES, total), bf16),
            pltpu.VMEM((8, lanes), f32),
        ],
        input_output_aliases={7: 0},
        compiler_params=pltpu.CompilerParams(vmem_limit_bytes=32 << 20),
        name="attend",
    )(starts, m_o, q_s, t_s, g_s, k, v, acc)


def close_tiles(acc_ref, low_t, b, tb, zp, bp):
    rows = low_t.shape[1]
    lanes = TILE * rows
    l3 = split2(low_t[0:16, :])
    lt3 = split2(low_t[16:32, :])
    llt = jnp.concatenate([lt3[0], lt3[0], lt3[1], l3[0], l3[0], l3[1]], axis=1)
    zz = jnp.zeros((16, rows), f32)
    for ti in range(acc_ref.shape[0]):
        a = acc_ref[ti]
        k0, k1, k2, k3 = (a[0:HS, n * lanes:(n + 1) * lanes] for n in range(4))
        l, aa, bb, cc = (a[HS:HS + 1, n * lanes:(n + 1) * lanes] for n in range(4))
        inv = 1.0 / l
        delta = aa * inv
        mt = bb * inv * SCALE
        dd = cc * inv * SCALE - mt * delta
        f = SCALE * inv
        grad = (k1 - delta * k0) * f
        gdot = (SCALE * (k3 - delta * k2) - mt * k1 + (mt * delta - dd) * k0) * f
        gh, gl = split2(grad)
        dh, dl = split2(gdot)
        for j in range(TILE):
            cols = slice((ti * TILE + j) * HS, (ti * TILE + j + 1) * HS)
            bj, tbj = b[:, cols], tb[:, cols]
            ln = slice(j * rows, (j + 1) * rows)
            zz += mm(jnp.concatenate([bj, bj, tbj, tbj], 1),
                     jnp.concatenate([dh[:, ln], dl[:, ln], gh[:, ln], gl[:, ln]], 0))
            r = jnp.concatenate([gh[:, ln], gl[:, ln], gh[:, ln], dh[:, ln], dl[:, ln], dh[:, ln]], axis=1)
            bp[ti * TILE + j] = mm(llt, r, NT)
    zp[...] = zz


from jax.sharding import PartitionSpec as P

MESH = pl.DeviceIdType.MESH
NX, NC, NZ = 4, 2, 4
GROUP = NX * NC


def place():
    ctx = lax.axis_index("ctx")
    return ctx, ctx // GROUP, (ctx // NC) % NX, ctx % NC


def at(z, x, core):
    return (z % NZ) * GROUP + (x % NX) * NC + core


def greet(ctx_peers, head_peers):
    barrier = pltpu.get_barrier_semaphore()
    for p in ctx_peers:
        pl.semaphore_signal(barrier, inc=1, device_id={"ctx": p}, device_id_type=MESH)
    for p in head_peers:
        pl.semaphore_signal(barrier, inc=1, device_id={"head": p}, device_id_type=MESH)
    return lambda: pl.semaphore_wait(barrier, len(ctx_peers) + len(head_peers))


def gather_kernel(n_head, k_ref, v_ref, x_ref, a_ref, ta_ref, qb_ref, cot_ref, b_ref, tb_ref, seg_ref, docs_ref,
                  kall, vall, low_ref, x_o, b_o, tb_o, starts_ref, q_s, t_s, g_s, acc_o, m_o,
                  qb_o, cot_o, s_own, kt, a_s, parts, mine, seg_s, docs_s, rk, rv, rl, ss, sl, loc):
    ctx, z, x, core = place()
    head = lax.axis_index("head")
    rows = k_ref.shape[0]
    heads = [lax.rem(head + d, n_head) for d in range(1, n_head)]
    twin = at(z, x, 1 - core)
    sides = [at(z, x + dx, core) for dx in (1, 3, 2)]
    ahead = [at(z + dz, x, core) for dz in range(NZ)]
    ready = greet(sides + ahead[1:] + [twin], heads)

    def cut(ref, j):
        return ref.at[pl.ds(pl.multiple_of(j * rows, rows), rows), :]

    pairs = [(x_ref, x_o), (a_ref, a_s.at[0:16]), (ta_ref, a_s.at[16:32]), (k_ref, cut(kall, ctx)), (v_ref, cut(vall, ctx)),
             (seg_ref, seg_s), (docs_ref, docs_s), (qb_ref, qb_o), (cot_ref, cot_o), (b_ref, b_o), (tb_ref, tb_o)]
    loads = [pltpu.make_async_copy(s, d, loc.at[i]) for i, (s, d) in enumerate(pairs)]
    for c in loads:
        c.start()
    for c in loads[:3]:
        c.wait()
    part = mm(a_s[...], x_o[...], NT)
    mine[...] = part
    parts[pl.ds(head, 1)] = part[None]
    ready()
    lows = []
    for i, p in enumerate(heads):
        c = pltpu.make_async_remote_copy(
            src_ref=mine, dst_ref=parts.at[head], send_sem=sl.at[i], recv_sem=rl.at[head],
            device_id={"head": p}, device_id_type=MESH)
        c.start()
        lows.append(c)

    sends = []
    count = [0]

    def push(kv, j, tos, cond=None, src=None):
        ref, sem = kv
        for to in tos:
            n = count[0]
            count[0] += 1

            def make(n=n, to=to):
                return pltpu.make_async_remote_copy(
                    src_ref=cut(ref, j) if src is None else src, dst_ref=cut(ref, j), send_sem=ss.at[n],
                    recv_sem=sem.at[j], device_id={"ctx": to}, device_id_type=MESH)

            make().start()
            sends.append((cond, make))

    K, V = (kall, rk), (vall, rv)

    def arrive(kv, j):
        ref, sem = kv
        pltpu.make_async_remote_copy(
            src_ref=cut(ref, j), dst_ref=cut(ref, j), send_sem=ss.at[0], recv_sem=sem.at[j],
            device_id={"ctx": twin}, device_id_type=MESH).wait_recv()

    def when(cond, f):
        if cond is None:
            f()
        else:
            pl.when(cond)(f)

    has = {0: None, 1: z >= 1, 2: z >= 2, 3: z >= 3}
    to1, to2, to3 = z <= 2, z <= 1, z == 0
    spot = [[at(z + NZ - d, x + dx, core) for dx in range(NX)] for d in range(NZ)]
    other = [[at(z + NZ - d, xx, 1 - core) for xx in range(NX)] for d in range(NZ)]

    for kv, src in ((K, k_ref), (V, v_ref)):
        when(to2, lambda: push(kv, ctx, [ahead[2]], to2, src))
        when(to1, lambda: push(kv, ctx, [ahead[1]], to1, src))
        push(kv, ctx, sides + [twin], None, src)
    for kv, src in ((K, k_ref), (V, v_ref)):
        when(to3, lambda: push(kv, ctx, [ahead[3]], to3, src))

    for c in loads[3:]:
        c.wait()
    seg = seg_s[...]
    starts = jnp.zeros(seg.shape, jnp.int32)
    for d in range(docs_s.shape[0]):
        starts = jnp.where(seg == d, docs_s[d], starts)
    starts_ref[...] = starts

    def row(d):
        for kv in (K, V):
            for dx in (1, 3, 2):
                arrive(kv, spot[d][dx])
                push(kv, spot[d][dx], [twin], has[d])

    def column(d):
        for kv in (K, V):
            arrive(kv, spot[d][0])
            push(kv, spot[d][0], sides + [twin], has[d])

    def low_sum():
        for i, p in enumerate(heads):
            pltpu.make_async_remote_copy(
                src_ref=mine, dst_ref=parts.at[p], send_sem=sl.at[i], recv_sem=rl.at[p],
                device_id={"head": p}, device_id_type=MESH).wait_recv()
        low_ref[...] = jnp.sum(parts[...], axis=0)

    def twins(d):
        for xx in range(NX):
            j = other[d][xx]
            arrive(K, j)
            arrive(V, j)

    when(has[1], lambda: column(1))
    row(0)
    low_sum()
    twins(0)
    span = GROUP * rows
    first = pl.multiple_of(z * span, span)
    kblk, vblk = kall.at[pl.ds(first, span), :], vall.at[pl.ds(first, span), :]
    kt[...] = transpose_keys(kblk[...])
    make_queries(low_ref[...], qb_o, cot_o, b_o[...], tb_o[...], q_s, t_s, g_s)

    def own(ti):
        own_tile(ti, first, ctx * rows, starts, kblk, vblk, kt, q_s, t_s, g_s, s_own, acc_o, m_o)

    own(0)
    when(has[2], lambda: column(2))
    when(has[3], lambda: column(3))
    own(1)
    when(has[1], lambda: row(1))
    own(2)
    own(3)
    when(has[2], lambda: row(2))
    when(has[3], lambda: row(3))
    for d in range(1, NZ):
        when(has[d], lambda: twins(d))
    groups = {}
    for cond, make in sends:
        groups.setdefault(id(cond), (cond, []))[1].append(make)

    def drain(makes):
        for make in makes:
            make().wait_send()

    for cond, makes in groups.values():
        when(cond, lambda: drain(makes))
    for c in lows:
        c.wait_send()


def gather(k, v, x, a_t, ta_t, qb, cot, b, tb, seg, docs, n_ctx, n_head):
    rows, width = k.shape
    vm = pl.BlockSpec(memory_space=pltpu.VMEM)
    hb = pl.BlockSpec(memory_space=pltpu.HBM)
    dma = pltpu.SemaphoreType.DMA
    like = jax.ShapeDtypeStruct
    args = (k, v, x, a_t, ta_t, qb, cot, b, tb, seg.reshape(1, rows), docs)
    n_q = qb.shape[1] // HS
    stack = like((n_q, rows, HS), bf16)
    lanes = TILE * rows
    return pl.pallas_call(
        functools.partial(gather_kernel, n_head),
        out_shape=(like((n_ctx * rows, width), bf16), like((n_ctx * rows, width), bf16), like((32, rows), f32),
                   like(x.shape, bf16), like(b.shape, bf16), like(tb.shape, bf16), like((1, rows), jnp.int32),
                   stack, stack, stack, like((n_q // TILE, HS + ONES, 4 * lanes), f32), like((n_q // TILE, 8, lanes), f32)),
        in_specs=[hb] * 11,
        out_specs=(vm,) * 12,
        scratch_shapes=[
            pltpu.VMEM(qb.shape, bf16),
            pltpu.VMEM(cot.shape, bf16),
            pltpu.VMEM((GROUP * rows, lanes), f32),
            pltpu.VMEM((HS + ONES, GROUP * rows), bf16),
            pltpu.VMEM((32, x.shape[1]), bf16),
            pltpu.VMEM((n_head, 32, rows), f32),
            pltpu.VMEM((32, rows), f32),
            pltpu.VMEM((1, rows), jnp.int32),
            pltpu.SMEM(docs.shape, jnp.int32),
            dma((n_ctx,)), dma((n_ctx,)), dma((n_head,)), dma((96,)), dma((n_head,)), dma((11,)),
        ],
        compiler_params=pltpu.CompilerParams(collective_id=0, has_side_effects=True, vmem_limit_bytes=20 << 20),
        name="gather",
    )(*(pltpu.with_memory_space_constraint(r, pltpu.HBM) for r in args))


def reduce_kernel(n_head, acc_ref, low_ref, b_ref, tb_ref, x_ref, oa_ref, ob_ref, zp_ref, zbuf, sa, sb, ra, rb, ca, cb, ta, tb,
                  rz, zs, rsa, rsb, ssa, ssb, rca, rcb, sca, scb, rga, rgb, sga, sgb):
    ctx, z, x, core = place()
    u = lax.rem(ctx, GROUP)
    head = lax.axis_index("head")
    heads = [lax.rem(head + d, n_head) for d in range(1, n_head)]
    mates = [lax.rem(u + d, GROUP) for d in range(1, GROUP)]
    cols = [lax.rem(z + d, NZ) for d in range(1, NZ)]
    ready = greet([z * GROUP + m for m in mates] + [c * GROUP + u for c in cols], heads)
    close_tiles(acc_ref, low_ref[...], b_ref[...], tb_ref[...], zp_ref, sb)
    zbuf[pl.ds(head, 1)] = zp_ref[...][None]
    ready()
    sends = []

    def copy(src, dst, ssem, rsem, dev):
        return pltpu.make_async_remote_copy(src_ref=src, dst_ref=dst, send_sem=ssem, recv_sem=rsem,
                                            device_id=dev, device_id_type=MESH)

    def start(c):
        c.start()
        sends.append(c)

    for i, p in enumerate(heads):
        start(copy(zp_ref, zbuf.at[head], zs.at[i], rz.at[head], {"head": p}))

    def scatter(s, r, ssem, rsem):
        for i, m in enumerate(mates):
            start(copy(s.at[m], r.at[u], ssem.at[i], rsem.at[u], {"ctx": z * GROUP + m}))
        r[pl.ds(u, 1)] = s[pl.ds(u, 1)]

    def across(r, c, s, rsem, ssem2, rsem2):
        for i, m in enumerate(mates):
            copy(r.at[m], r.at[m], ssem2.at[0], rsem.at[m], {"ctx": z * GROUP + m}).wait_recv()
        part = jnp.sum(r[...], axis=0)
        s[...] = part
        c[pl.ds(z, 1)] = part[None]
        for i, q in enumerate(cols):
            start(copy(s, c.at[z], ssem2.at[i], rsem2.at[z], {"ctx": q * GROUP + u}))

    def spread(c, t, o, ssem, rsem, ssem2, rsem2):
        for i, q in enumerate(cols):
            copy(t.at[q], c.at[q], ssem.at[0], rsem.at[q], {"ctx": q * GROUP + u}).wait_recv()
        t[pl.ds(u, 1)] = jnp.sum(c[...], axis=0)[None]
        for i, m in enumerate(mates):
            start(copy(t.at[u], t.at[u], ssem2.at[i], rsem2.at[u], {"ctx": z * GROUP + m}))

    def collect(t, o, ssem, rsem):
        for m in mates:
            copy(t.at[m], t.at[m], ssem.at[0], rsem.at[m], {"ctx": z * GROUP + m}).wait_recv()
        for i in range(GROUP):
            o[:, i * HS:(i + 1) * HS] = t[i]

    scatter(sb, rb, ssb, rsb)
    for i, p in enumerate(heads):
        copy(zp_ref, zbuf.at[p], zs.at[0], rz.at[p], {"head": p}).wait_recv()
    zsum = jnp.sum(zbuf[...], axis=0)
    ap = mm(jnp.concatenate(split3(zsum), 0), x_ref[...])
    ap = ap[0:16] + ap[16:32] + ap[32:48]
    for i in range(GROUP):
        sa[i] = ap[:, i * HS:(i + 1) * HS]
    scatter(sa, ra, ssa, rsa)
    across(rb, cb, sb_part(sb), rsb, scb, rcb)
    across(ra, ca, sb_part(sa), rsa, sca, rca)
    spread(cb, tb, ob_ref, scb, rcb, sgb, rgb)
    spread(ca, ta, oa_ref, sca, rca, sga, rga)
    collect(tb, ob_ref, sgb, rgb)
    collect(ta, oa_ref, sga, rga)
    for c in sends:
        c.wait_send()


def sb_part(s):
    return s.at[GROUP]


def reduce(acc, low_t, b, tb, x, n_head):
    width = b.shape[1]
    rows = low_t.shape[1]
    vm = pl.BlockSpec(memory_space=pltpu.VMEM)
    out = jax.ShapeDtypeStruct((16, width), f32)
    dma = pltpu.SemaphoreType.DMA
    return pl.pallas_call(
        functools.partial(reduce_kernel, n_head),
        out_shape=(out, out),
        in_specs=[vm] * 5,
        out_specs=(vm, vm),
        scratch_shapes=[
            pltpu.VMEM((16, rows), f32),
            pltpu.VMEM((n_head, 16, rows), f32),
            pltpu.VMEM((GROUP + 1, 16, HS), f32), pltpu.VMEM((GROUP + 1, 16, HS), f32),
            pltpu.VMEM((GROUP, 16, HS), f32), pltpu.VMEM((GROUP, 16, HS), f32),
            pltpu.VMEM((NZ, 16, HS), f32), pltpu.VMEM((NZ, 16, HS), f32),
            pltpu.VMEM((GROUP, 16, HS), f32), pltpu.VMEM((GROUP, 16, HS), f32),
            dma((n_head,)), dma((n_head,)),
            dma((GROUP,)), dma((GROUP,)), dma((GROUP,)), dma((GROUP,)),
            dma((NZ,)), dma((NZ,)), dma((NZ,)), dma((NZ,)),
            dma((GROUP,)), dma((GROUP,)), dma((GROUP,)), dma((GROUP,)),
        ],
        compiler_params=pltpu.CompilerParams(collective_id=1, has_side_effects=True, vmem_limit_bytes=6 << 20),
        name="reduce",
    )(acc, low_t, b, tb, x)


def finish_kernel(a_ref, b_ref, oa_ref, ob_ref, sem):
    copies = [pltpu.make_async_copy(a_ref, oa_ref, sem.at[0]), pltpu.make_async_copy(b_ref, ob_ref, sem.at[1])]
    for c in copies:
        c.start()
    for c in copies:
        c.wait()


def finish(a, b):
    vm = pl.BlockSpec(memory_space=pltpu.VMEM)
    hb = pl.BlockSpec(memory_space=pltpu.HBM)
    return pl.pallas_call(
        finish_kernel,
        out_shape=(jax.ShapeDtypeStruct(a.shape, f32), jax.ShapeDtypeStruct(b.shape, f32)),
        in_specs=[vm, vm],
        out_specs=(hb, hb),
        scratch_shapes=[pltpu.SemaphoreType.DMA((2,))],
        compiler_params=pltpu.CompilerParams(vmem_limit_bytes=1 << 20),
        name="finish",
    )(a, b)


def on_device(n_ctx, n_head, activations, query_base, key_rows, values, out_cotangent, adapter_a, adapter_b, tangent_a, tangent_b,
              segment_ids, doc_starts):
    rows = activations.shape[0]
    kall, vall, low_t, x, b, tb, starts, q_s, t_s, g_s, acc, m_o = gather(
        key_rows, values, activations, adapter_a.T, tangent_a.T, query_base, out_cotangent, adapter_b, tangent_b,
        segment_ids, doc_starts, n_ctx, n_head)
    acc = attend(starts, m_o, q_s, t_s, g_s, kall, vall, acc, lambda: lax.axis_index("ctx") // GROUP, GROUP * rows)
    oa, ob = finish(*reduce(acc, low_t, b, tb, x, n_head))
    return oa.T, ob


def solution(mesh):
    wide = P("ctx", "head")
    placed = (wide,) * 5 + (P("head", None), P(None, "head"), P("head", None), P(None, "head"), P("ctx"), P())
    return jax.shard_map(
        functools.partial(on_device, mesh.shape["ctx"], mesh.shape["head"]),
        mesh=mesh,
        in_specs=placed,
        out_specs=(P("head", None), P(None, "head")),
        check_vma=False,
    )
```

```python
import functools, math
import jax, jax.numpy as jnp
from jax import lax
from jax.experimental import pallas as pl
from jax.experimental.pallas import tpu as pltpu

HS = 128
TILE = 2
ONES = 16
NT = (((1,), (1,)), ((), ()))
TN = (((0,), (0,)), ((), ()))
NN = (((1,), (0,)), ((), ()))
f32, bf16 = jnp.float32, jnp.bfloat16
SCALE = 1.0 / math.sqrt(HS)
CEXP = SCALE * math.log2(math.e)


def mm(a, b, dims=NN):
    return lax.dot_general(a, b, dims, preferred_element_type=f32)


def split2(x):
    hi = x.astype(bf16)
    return hi, (x - hi.astype(f32)).astype(bf16)


def split3(x):
    hi = x.astype(bf16)
    r = x - hi.astype(f32)
    mid = r.astype(bf16)
    return hi, mid, (r - mid.astype(f32)).astype(bf16)


def make_queries(low_t, qb_ref, cot_ref, b, tb, q_s, t_s, g_s):
    l3 = split3(low_t[0:16, :])
    lt3 = split3(low_t[16:32, :])
    q_all = mm(jnp.concatenate(l3, 0), jnp.concatenate([b, b, b], 0), TN) + qb_ref[...].astype(f32)
    t_all = mm(jnp.concatenate(lt3 + l3, 0), jnp.concatenate([b, b, b, tb, tb, tb], 0), TN)
    for h in range(q_s.shape[0]):
        cols = slice(h * HS, (h + 1) * HS)
        q_s[h] = q_all[:, cols].astype(bf16)
        t_s[h] = t_all[:, cols].astype(bf16)
        g_s[h] = cot_ref[:, cols]


def pick(ref, ti):
    v = ref[pl.ds(ti * TILE, TILE)]
    return v.reshape(TILE * v.shape[1], HS)


def weights(s, mc, kblk, vblk, t2, g2):
    e = jnp.exp2(s * CEXP - mc)
    t = mm(kblk, t2, NT)
    p = mm(vblk, g2, NT)
    w1 = e * p
    w2 = e * t
    w3 = w1 * t
    return jnp.concatenate([e.astype(bf16), w1.astype(bf16), w2.astype(bf16), w3.astype(bf16)], axis=1)


def transpose_keys(kblk):
    return jnp.concatenate([kblk.T, jnp.ones((ONES, kblk.shape[0]), bf16)], axis=0)


def own_tile(ti, first, base, starts, kblk, vblk, kt, q_s, t_s, g_s, s_own, acc_o, m_o):
    rows = starts.shape[1]
    n_keys = kblk.shape[0]
    lead = pl.ds(0, n_keys)
    pos = base + lax.broadcasted_iota(jnp.int32, (1, rows), 1)
    starts2 = jnp.concatenate([starts] * TILE, axis=1)
    pos2 = jnp.concatenate([pos] * TILE, axis=1)
    s = mm(kblk[...], pick(q_s, ti), NT)
    kp = first + lax.broadcasted_iota(jnp.int32, s.shape, 0)
    s = jnp.where((kp >= starts2) & (kp <= pos2), s, -1e30)
    s_own[lead, :] = s
    m = jnp.max(jnp.max(s.reshape(n_keys // 8, 8, s.shape[1]), axis=0), axis=0, keepdims=True)
    m_o[ti] = jnp.broadcast_to(m, m_o.shape[1:])
    w = weights(s_own[lead, :], m * CEXP, kblk[...], vblk[...], pick(t_s, ti), pick(g_s, ti))
    acc_o[ti] = mm(kt[:, lead], w)


def prev_tile(ti, first, starts, kblk, vblk, kt, q_s, t_s, g_s, s_own, acc_i, acc_o, m_i, m_o):
    n_keys = kblk.shape[0]
    starts2 = jnp.concatenate([starts] * TILE, axis=1)
    s = mm(kblk[...], pick(q_s, ti), NT)
    kp = first + lax.broadcasted_iota(jnp.int32, s.shape, 0)
    s = jnp.where(kp >= starts2, s, -1e30)
    s_own[...] = s
    m_old = m_i[ti][0:1]
    m = jnp.max(jnp.max(s.reshape(n_keys // 8, 8, s.shape[1]), axis=0), axis=0, keepdims=True)
    mc = jnp.maximum(m_old, m) * CEXP
    if m_o is not None:
        m_o[ti] = jnp.broadcast_to(jnp.maximum(m_old, m), m_o.shape[1:])
    factor = jnp.exp2(m_old * CEXP - mc)
    w = weights(s_own[...], mc, kblk[...], vblk[...], pick(t_s, ti), pick(g_s, ti))
    acc_o[ti] = acc_i[ti] * jnp.concatenate([factor] * 4, axis=1) + mm(kt[...], w)


def attend_kernel(kb_len, own_fn, starts_ref, q_s, t_s, g_s, k_ref, v_ref, m_in, acc_in, m_ref, acc, s_buf, kt, m_new):
    lanes = TILE * starts_ref.shape[1]
    starts = starts_ref[...]
    start_last = jnp.max(starts)
    lo = jnp.min(starts) // kb_len
    hi = own_fn()
    starts2 = jnp.concatenate([starts] * TILE, axis=1)

    def build(kb, c):
        off = pl.multiple_of(kb * kb_len, kb_len)
        kt[:, pl.ds(off, kb_len)] = transpose_keys(k_ref[pl.ds(off, kb_len), :])
        return c

    lax.fori_loop(lo, hi, build, 0)

    def one_tile(ti, carry):
        q2, t2, g2 = pick(q_s, ti), pick(t_s, ti), pick(g_s, ti)
        m_old = m_ref[ti]
        m_new[...] = m_old

        def pass1(kb, c):
            off = pl.multiple_of(kb * kb_len, kb_len)

            def keep(s):
                s_buf[pl.ds(off, kb_len), :] = s
                m_new[...] = jnp.maximum(m_new[...], jnp.max(s.reshape(kb_len // 8, 8, lanes), axis=0))

            @pl.when(off < start_last)
            def _():
                s = mm(k_ref[pl.ds(off, kb_len), :], q2, NT)
                kp = off + lax.broadcasted_iota(jnp.int32, (kb_len, lanes), 0)
                keep(jnp.where(kp >= starts2, s, -1e30))

            @pl.when(off >= start_last)
            def _():
                keep(mm(k_ref[pl.ds(off, kb_len), :], q2, NT))
            return c

        lax.fori_loop(lo, hi, pass1, 0)
        m = jnp.max(m_new[...], axis=0, keepdims=True)
        mc = m * CEXP
        factor = jnp.exp2(m_old[0:1] * CEXP - mc)
        acc[ti] = acc[ti] * jnp.concatenate([factor] * 4, axis=1)
        m_ref[ti] = jnp.broadcast_to(m, m_new.shape)

        def pass2(kb, c):
            off = pl.multiple_of(kb * kb_len, kb_len)
            w = weights(s_buf[pl.ds(off, kb_len), :], mc, k_ref[pl.ds(off, kb_len), :], v_ref[pl.ds(off, kb_len), :], t2, g2)
            acc[ti] += mm(kt[:, pl.ds(off, kb_len)], w)
            return c

        lax.fori_loop(lo, hi, pass2, 0)
        return carry

    lax.fori_loop(0, jnp.where(lo < hi, acc.shape[0], 0), one_tile, 0)


def attend(starts, m_o, q_s, t_s, g_s, k, v, acc, own_fn, kb_len):
    total = k.shape[0]
    lanes = TILE * starts.shape[1]
    vm = pl.BlockSpec(memory_space=pltpu.VMEM)
    return pl.pallas_call(
        functools.partial(attend_kernel, kb_len, own_fn),
        out_shape=(jax.ShapeDtypeStruct(m_o.shape, f32), jax.ShapeDtypeStruct(acc.shape, f32)),
        in_specs=[vm] * 8,
        out_specs=(vm, vm),
        scratch_shapes=[
            pltpu.VMEM((total, lanes), f32),
            pltpu.VMEM((HS + ONES, total), bf16),
            pltpu.VMEM((8, lanes), f32),
        ],
        input_output_aliases={6: 0, 7: 1},
        compiler_params=pltpu.CompilerParams(vmem_limit_bytes=32 << 20),
        name="attend",
    )(starts, q_s, t_s, g_s, k, v, m_o, acc)


def close_tiles(acc_ref, accs, low_t, b, tb, zp, bp):
    rows = low_t.shape[1]
    lanes = TILE * rows
    l3 = split2(low_t[0:16, :])
    lt3 = split2(low_t[16:32, :])
    llt = jnp.concatenate([lt3[0], lt3[0], lt3[1], l3[0], l3[0], l3[1]], axis=1)
    zz = jnp.zeros((16, rows), f32)
    for ti in range(acc_ref.shape[0]):
        a = acc_ref[ti] if ti < LATE else accs[ti - LATE]
        k0, k1, k2, k3 = (a[0:HS, n * lanes:(n + 1) * lanes] for n in range(4))
        l, aa, bb, cc = (a[HS:HS + 1, n * lanes:(n + 1) * lanes] for n in range(4))
        inv = 1.0 / l
        delta = aa * inv
        mt = bb * inv * SCALE
        dd = cc * inv * SCALE - mt * delta
        f = SCALE * inv
        grad = (k1 - delta * k0) * f
        gdot = (SCALE * (k3 - delta * k2) - mt * k1 + (mt * delta - dd) * k0) * f
        gh, gl = split2(grad)
        dh, dl = split2(gdot)
        for j in range(TILE):
            cols = slice((ti * TILE + j) * HS, (ti * TILE + j + 1) * HS)
            bj, tbj = b[:, cols], tb[:, cols]
            ln = slice(j * rows, (j + 1) * rows)
            zz += mm(jnp.concatenate([bj, bj, tbj, tbj], 1),
                     jnp.concatenate([dh[:, ln], dl[:, ln], gh[:, ln], gl[:, ln]], 0))
            r = jnp.concatenate([gh[:, ln], gl[:, ln], gh[:, ln], dh[:, ln], dl[:, ln], dh[:, ln]], axis=1)
            bp[ti * TILE + j] = mm(llt, r, NT)
    zp[...] = zz


from jax.sharding import PartitionSpec as P

MESH = pl.DeviceIdType.MESH
LATE = 3


class Shifted:
    def __init__(self, ref, by):
        self.ref, self.by = ref, by

    def __setitem__(self, i, v):
        self.ref[i - self.by] = v

NX, NC, NZ = 4, 2, 4
GROUP = NX * NC


def place():
    ctx = lax.axis_index("ctx")
    return ctx, ctx // GROUP, (ctx // NC) % NX, ctx % NC


def at(z, x, core):
    return (z % NZ) * GROUP + (x % NX) * NC + core


def greet(ctx_peers, head_peers):
    barrier = pltpu.get_barrier_semaphore()
    for p in ctx_peers:
        pl.semaphore_signal(barrier, inc=1, device_id={"ctx": p}, device_id_type=MESH)
    for p in head_peers:
        pl.semaphore_signal(barrier, inc=1, device_id={"head": p}, device_id_type=MESH)
    return lambda: pl.semaphore_wait(barrier, len(ctx_peers) + len(head_peers))


def gather_kernel(n_head, k_ref, v_ref, x_ref, a_ref, ta_ref, qb_ref, cot_ref, b_ref, tb_ref, seg_ref, docs_ref,
                  kall, vall, low_ref, x_o, b_o, tb_o, starts_ref, q_s, t_s, g_s, acc_o, m_o,
                  qb_o, cot_o, s_own, kt, a_s, parts, mine, seg_s, docs_s, rk, rv, rl, ss, sl, loc):
    ctx, z, x, core = place()
    head = lax.axis_index("head")
    rows = k_ref.shape[0]
    heads = [lax.rem(head + d, n_head) for d in range(1, n_head)]
    twin = at(z, x, 1 - core)
    sides = [at(z, x + dx, core) for dx in (1, 3, 2)]
    ahead = [at(z + dz, x, core) for dz in range(NZ)]
    ready = greet(sides + [ahead[1], ahead[3], twin], heads)

    def cut(ref, j):
        return ref.at[pl.ds(pl.multiple_of(j * rows, rows), rows), :]

    pairs = [(x_ref, x_o), (a_ref, a_s.at[0:16]), (ta_ref, a_s.at[16:32]), (k_ref, cut(kall, ctx)), (v_ref, cut(vall, ctx)),
             (seg_ref, seg_s), (docs_ref, docs_s), (qb_ref, qb_o), (cot_ref, cot_o), (b_ref, b_o), (tb_ref, tb_o)]
    loads = [pltpu.make_async_copy(s, d, loc.at[i]) for i, (s, d) in enumerate(pairs)]
    for c in loads:
        c.start()
    for c in loads[:3]:
        c.wait()
    part = mm(a_s[...], x_o[...], NT)
    mine[...] = part
    parts[pl.ds(head, 1)] = part[None]
    ready()
    lows = []
    for i, p in enumerate(heads):
        c = pltpu.make_async_remote_copy(
            src_ref=mine, dst_ref=parts.at[head], send_sem=sl.at[i], recv_sem=rl.at[head],
            device_id={"head": p}, device_id_type=MESH)
        c.start()
        lows.append(c)

    sends = []
    count = [0]

    def push(kv, j, tos, cond=None, src=None):
        ref, sem = kv
        for to in tos:
            n = count[0]
            count[0] += 1

            def make(n=n, to=to):
                return pltpu.make_async_remote_copy(
                    src_ref=cut(ref, j) if src is None else src, dst_ref=cut(ref, j), send_sem=ss.at[n],
                    recv_sem=sem.at[j], device_id={"ctx": to}, device_id_type=MESH)

            make().start()
            sends.append((cond, make))

    K, V = (kall, rk), (vall, rv)

    def arrive(kv, j):
        ref, sem = kv
        pltpu.make_async_remote_copy(
            src_ref=cut(ref, j), dst_ref=cut(ref, j), send_sem=ss.at[0], recv_sem=sem.at[j],
            device_id={"ctx": twin}, device_id_type=MESH).wait_recv()

    def when(cond, f):
        if cond is None:
            f()
        else:
            pl.when(cond)(f)

    has = {0: None, 1: z >= 1, 2: z >= 2, 3: z >= 3}
    to1, to3, both = z <= 2, z == 0, (z >= 1) & (z <= 2)
    spot = [[at(z + NZ - d, x + dx, core) for dx in range(NX)] for d in range(NZ)]
    other = [[at(z + NZ - d, xx, 1 - core) for xx in range(NX)] for d in range(NZ)]

    for kv, src in ((K, k_ref), (V, v_ref)):
        when(to1, lambda: push(kv, ctx, [ahead[1]], to1, src))
        push(kv, ctx, sides + [twin], None, src)
    for kv, src in ((K, k_ref), (V, v_ref)):
        when(to3, lambda: push(kv, ctx, [ahead[3]], to3, src))

    for c in loads[3:]:
        c.wait()
    seg = seg_s[...]
    starts = jnp.zeros(seg.shape, jnp.int32)
    for d in range(docs_s.shape[0]):
        starts = jnp.where(seg == d, docs_s[d], starts)
    starts_ref[...] = starts

    def row(d):
        for kv in (K, V):
            for dx in (1, 3, 2):
                arrive(kv, spot[d][dx])
                push(kv, spot[d][dx], [twin], has[d])

    def column(d):
        for kv in (K, V):
            arrive(kv, spot[d][0])
            if d == 1:
                when(both, lambda: push(kv, spot[d][0], [ahead[1]], both))
            push(kv, spot[d][0], sides + [twin], has[d])

    def low_sum():
        for i, p in enumerate(heads):
            pltpu.make_async_remote_copy(
                src_ref=mine, dst_ref=parts.at[p], send_sem=sl.at[i], recv_sem=rl.at[p],
                device_id={"head": p}, device_id_type=MESH).wait_recv()
        low_ref[...] = jnp.sum(parts[...], axis=0)

    def twins(d):
        for xx in range(NX):
            j = other[d][xx]
            arrive(K, j)
            arrive(V, j)

    when(has[1], lambda: column(1))
    row(0)
    low_sum()
    make_queries(low_ref[...], qb_o, cot_o, b_o[...], tb_o[...], q_s, t_s, g_s)
    twins(0)
    span = GROUP * rows
    first = pl.multiple_of(z * span, span)
    kblk, vblk = kall.at[pl.ds(first, span), :], vall.at[pl.ds(first, span), :]
    kt[...] = transpose_keys(kblk[...])

    u = lax.rem(ctx, GROUP)

    def own(ti):
        for low_u, high_u in ((0, 4), (4, 6), (6, 8)):
            @pl.when((u >= low_u) & (u < high_u))
            def _():
                n = high_u * rows
                kb, vb = kall.at[pl.ds(first, n), :], vall.at[pl.ds(first, n), :]
                own_tile(ti, first, ctx * rows, starts, kb, vb, kt, q_s, t_s, g_s, s_own, acc_o, m_o)

    own(0)
    own(1)
    when(has[2], lambda: column(2))
    when(has[3], lambda: column(3))
    own(2)
    when(has[1], lambda: row(1))
    own(3)
    when(has[1], lambda: twins(1))
    back = pl.multiple_of(jnp.maximum(z - 1, 0) * span, span)
    kpre, vpre = kall.at[pl.ds(back, span), :], vall.at[pl.ds(back, span), :]

    def older(lo, hi):
        for ti in range(lo, hi):
            prev_tile(ti, back, starts, kpre, vpre, kt, q_s, t_s, g_s, s_own, acc_o, acc_o, m_o, m_o)

    def older_first():
        kt[...] = transpose_keys(kpre[...])
        older(0, 2)

    when(has[1], older_first)
    when(has[2], lambda: row(2))
    when(has[3], lambda: row(3))
    when(has[1], lambda: older(2, LATE))
    for d in range(2, NZ):
        when(has[d], lambda: twins(d))
    groups = {}
    for cond, make in sends:
        groups.setdefault(id(cond), (cond, []))[1].append(make)

    def drain(makes):
        for make in makes:
            make().wait_send()

    for cond, makes in groups.values():
        when(cond, lambda: drain(makes))
    for c in lows:
        c.wait_send()


def gather(k, v, x, a_t, ta_t, qb, cot, b, tb, seg, docs, n_ctx, n_head):
    rows, width = k.shape
    vm = pl.BlockSpec(memory_space=pltpu.VMEM)
    hb = pl.BlockSpec(memory_space=pltpu.HBM)
    dma = pltpu.SemaphoreType.DMA
    like = jax.ShapeDtypeStruct
    args = (k, v, x, a_t, ta_t, qb, cot, b, tb, seg.reshape(1, rows), docs)
    n_q = qb.shape[1] // HS
    stack = like((n_q, rows, HS), bf16)
    lanes = TILE * rows
    return pl.pallas_call(
        functools.partial(gather_kernel, n_head),
        out_shape=(like((n_ctx * rows, width), bf16), like((n_ctx * rows, width), bf16), like((32, rows), f32),
                   like(x.shape, bf16), like(b.shape, bf16), like(tb.shape, bf16), like((1, rows), jnp.int32),
                   stack, stack, stack, like((n_q // TILE, HS + ONES, 4 * lanes), f32), like((n_q // TILE, 8, lanes), f32)),
        in_specs=[hb] * 11,
        out_specs=(vm,) * 12,
        scratch_shapes=[
            pltpu.VMEM(qb.shape, bf16),
            pltpu.VMEM(cot.shape, bf16),
            pltpu.VMEM((GROUP * rows, lanes), f32),
            pltpu.VMEM((HS + ONES, GROUP * rows), bf16),
            pltpu.VMEM((32, x.shape[1]), bf16),
            pltpu.VMEM((n_head, 32, rows), f32),
            pltpu.VMEM((32, rows), f32),
            pltpu.VMEM((1, rows), jnp.int32),
            pltpu.SMEM(docs.shape, jnp.int32),
            dma((n_ctx,)), dma((n_ctx,)), dma((n_head,)), dma((96,)), dma((n_head,)), dma((11,)),
        ],
        compiler_params=pltpu.CompilerParams(collective_id=0, has_side_effects=True, vmem_limit_bytes=20 << 20),
        name="gather",
    )(*(pltpu.with_memory_space_constraint(r, pltpu.HBM) for r in args))


def reduce_kernel(n_head, acc_ref, m_ref, starts_ref, kall, vall, q_s, t_s, g_s, low_ref, b_ref, tb_ref, x_ref, oa_ref, ob_ref,
                  accs, kt, s_own, zp_ref, zbuf, sa, sb, ra, rb, ca, cb, ta, tb,
                  rz, zs, rsa, rsb, ssa, ssb, rca, rcb, sca, scb, rga, rgb, sga, sgb):
    ctx, z, x, core = place()
    u = lax.rem(ctx, GROUP)
    head = lax.axis_index("head")
    heads = [lax.rem(head + d, n_head) for d in range(1, n_head)]
    mates = [lax.rem(u + d, GROUP) for d in range(1, GROUP)]
    cols = [lax.rem(z + d, NZ) for d in range(1, NZ)]
    ready = greet([z * GROUP + m for m in mates] + [c * GROUP + u for c in cols], heads)
    accs[...] = acc_ref[LATE:]

    @pl.when(z >= 1)
    def _():
        span = GROUP * x_ref.shape[0]
        back = pl.multiple_of(jnp.maximum(z - 1, 0) * span, span)
        kpre, vpre = kall.at[pl.ds(back, span), :], vall.at[pl.ds(back, span), :]
        kt[...] = transpose_keys(kpre[...])
        for ti in range(LATE, acc_ref.shape[0]):
            prev_tile(ti, back, starts_ref[...], kpre, vpre, kt, q_s, t_s, g_s, s_own, acc_ref,
                      Shifted(accs, LATE), m_ref, None)

    close_tiles(acc_ref, accs, low_ref[...], b_ref[...], tb_ref[...], zp_ref, sb)
    zbuf[pl.ds(head, 1)] = zp_ref[...][None]
    ready()
    sends = []

    def copy(src, dst, ssem, rsem, dev):
        return pltpu.make_async_remote_copy(src_ref=src, dst_ref=dst, send_sem=ssem, recv_sem=rsem,
                                            device_id=dev, device_id_type=MESH)

    def start(c):
        c.start()
        sends.append(c)

    for i, p in enumerate(heads):
        start(copy(zp_ref, zbuf.at[head], zs.at[i], rz.at[head], {"head": p}))

    def scatter(s, r, ssem, rsem):
        for i, m in enumerate(mates):
            start(copy(s.at[m], r.at[u], ssem.at[i], rsem.at[u], {"ctx": z * GROUP + m}))
        r[pl.ds(u, 1)] = s[pl.ds(u, 1)]

    def across(r, c, s, rsem, ssem2, rsem2):
        for i, m in enumerate(mates):
            copy(r.at[m], r.at[m], ssem2.at[0], rsem.at[m], {"ctx": z * GROUP + m}).wait_recv()
        part = jnp.sum(r[...], axis=0)
        s[...] = part
        c[pl.ds(z, 1)] = part[None]
        for i, q in enumerate(cols):
            start(copy(s, c.at[z], ssem2.at[i], rsem2.at[z], {"ctx": q * GROUP + u}))

    def spread(c, t, o, ssem, rsem, ssem2, rsem2):
        for i, q in enumerate(cols):
            copy(t.at[q], c.at[q], ssem.at[0], rsem.at[q], {"ctx": q * GROUP + u}).wait_recv()
        t[pl.ds(u, 1)] = jnp.sum(c[...], axis=0)[None]
        for i, m in enumerate(mates):
            start(copy(t.at[u], t.at[u], ssem2.at[i], rsem2.at[u], {"ctx": z * GROUP + m}))

    def collect(t, o, ssem, rsem):
        for m in mates:
            copy(t.at[m], t.at[m], ssem.at[0], rsem.at[m], {"ctx": z * GROUP + m}).wait_recv()
        for i in range(GROUP):
            o[:, i * HS:(i + 1) * HS] = t[i]

    scatter(sb, rb, ssb, rsb)
    for i, p in enumerate(heads):
        copy(zp_ref, zbuf.at[p], zs.at[0], rz.at[p], {"head": p}).wait_recv()
    zsum = jnp.sum(zbuf[...], axis=0)
    ap = mm(jnp.concatenate(split3(zsum), 0), x_ref[...])
    ap = ap[0:16] + ap[16:32] + ap[32:48]
    for i in range(GROUP):
        sa[i] = ap[:, i * HS:(i + 1) * HS]
    scatter(sa, ra, ssa, rsa)
    across(rb, cb, sb_part(sb), rsb, scb, rcb)
    across(ra, ca, sb_part(sa), rsa, sca, rca)
    spread(cb, tb, ob_ref, scb, rcb, sgb, rgb)
    spread(ca, ta, oa_ref, sca, rca, sga, rga)
    collect(tb, ob_ref, sgb, rgb)
    collect(ta, oa_ref, sga, rga)
    for c in sends:
        c.wait_send()


def sb_part(s):
    return s.at[GROUP]


def reduce(acc, m_o, starts, kall, vall, q_s, t_s, g_s, low_t, b, tb, x, n_head):
    width = b.shape[1]
    rows = low_t.shape[1]
    vm = pl.BlockSpec(memory_space=pltpu.VMEM)
    out = jax.ShapeDtypeStruct((16, width), f32)
    dma = pltpu.SemaphoreType.DMA
    return pl.pallas_call(
        functools.partial(reduce_kernel, n_head),
        out_shape=(out, out),
        in_specs=[vm] * 12,
        out_specs=(vm, vm),
        scratch_shapes=[
            pltpu.VMEM((acc.shape[0] - LATE,) + acc.shape[1:], f32),
            pltpu.VMEM((HS + ONES, GROUP * rows), bf16),
            pltpu.VMEM((GROUP * rows, TILE * rows), f32),
            pltpu.VMEM((16, rows), f32),
            pltpu.VMEM((n_head, 16, rows), f32),
            pltpu.VMEM((GROUP + 1, 16, HS), f32), pltpu.VMEM((GROUP + 1, 16, HS), f32),
            pltpu.VMEM((GROUP, 16, HS), f32), pltpu.VMEM((GROUP, 16, HS), f32),
            pltpu.VMEM((NZ, 16, HS), f32), pltpu.VMEM((NZ, 16, HS), f32),
            pltpu.VMEM((GROUP, 16, HS), f32), pltpu.VMEM((GROUP, 16, HS), f32),
            dma((n_head,)), dma((n_head,)),
            dma((GROUP,)), dma((GROUP,)), dma((GROUP,)), dma((GROUP,)),
            dma((NZ,)), dma((NZ,)), dma((NZ,)), dma((NZ,)),
            dma((GROUP,)), dma((GROUP,)), dma((GROUP,)), dma((GROUP,)),
        ],
        compiler_params=pltpu.CompilerParams(collective_id=1, has_side_effects=True, vmem_limit_bytes=12 << 20),
        name="reduce",
    )(acc, m_o, starts, kall, vall, q_s, t_s, g_s, low_t, b, tb, x)


def finish_kernel(a_ref, b_ref, oa_ref, ob_ref, sem):
    copies = [pltpu.make_async_copy(a_ref, oa_ref, sem.at[0]), pltpu.make_async_copy(b_ref, ob_ref, sem.at[1])]
    for c in copies:
        c.start()
    for c in copies:
        c.wait()


def finish(a, b):
    vm = pl.BlockSpec(memory_space=pltpu.VMEM)
    hb = pl.BlockSpec(memory_space=pltpu.HBM)
    return pl.pallas_call(
        finish_kernel,
        out_shape=(jax.ShapeDtypeStruct(a.shape, f32), jax.ShapeDtypeStruct(b.shape, f32)),
        in_specs=[vm, vm],
        out_specs=(hb, hb),
        scratch_shapes=[pltpu.SemaphoreType.DMA((2,))],
        compiler_params=pltpu.CompilerParams(vmem_limit_bytes=1 << 20),
        name="finish",
    )(a, b)


def on_device(n_ctx, n_head, activations, query_base, key_rows, values, out_cotangent, adapter_a, adapter_b, tangent_a, tangent_b,
              segment_ids, doc_starts):
    rows = activations.shape[0]
    kall, vall, low_t, x, b, tb, starts, q_s, t_s, g_s, acc, m_o = gather(
        key_rows, values, activations, adapter_a.T, tangent_a.T, query_base, out_cotangent, adapter_b, tangent_b,
        segment_ids, doc_starts, n_ctx, n_head)
    m_o, acc = attend(starts, m_o, q_s, t_s, g_s, kall, vall, acc, lambda: jnp.maximum(lax.axis_index("ctx") // GROUP - 1, 0), GROUP * rows)
    oa, ob = finish(*reduce(acc, m_o, starts, kall, vall, q_s, t_s, g_s, low_t, b, tb, x, n_head))
    return oa.T, ob


def solution(mesh):
    wide = P("ctx", "head")
    placed = (wide,) * 5 + (P("head", None), P(None, "head"), P("head", None), P(None, "head"), P("ctx"), P())
    return jax.shard_map(
        functools.partial(on_device, mesh.shape["ctx"], mesh.shape["head"]),
        mesh=mesh,
        in_specs=placed,
        out_specs=(P("head", None), P(None, "head")),
        check_vma=False,
    )
```

```python
import functools, math
import jax, jax.numpy as jnp
from jax import lax
from jax.experimental import pallas as pl
from jax.experimental.pallas import tpu as pltpu

HS = 128
TILE = 2
ONES = 16
NT = (((1,), (1,)), ((), ()))
TN = (((0,), (0,)), ((), ()))
NN = (((1,), (0,)), ((), ()))
f32, bf16 = jnp.float32, jnp.bfloat16
SCALE = 1.0 / math.sqrt(HS)
CEXP = SCALE * math.log2(math.e)


def mm(a, b, dims=NN):
    return lax.dot_general(a, b, dims, preferred_element_type=f32)


def split2(x):
    hi = x.astype(bf16)
    return hi, (x - hi.astype(f32)).astype(bf16)


def split3(x):
    hi = x.astype(bf16)
    r = x - hi.astype(f32)
    mid = r.astype(bf16)
    return hi, mid, (r - mid.astype(f32)).astype(bf16)


def make_queries(low_t, qb_ref, cot_ref, b, tb, q_s, t_s, g_s):
    l3 = split3(low_t[0:16, :])
    lt3 = split3(low_t[16:32, :])
    q_all = mm(jnp.concatenate(l3, 0), jnp.concatenate([b, b, b], 0), TN) + qb_ref[...].astype(f32)
    t_all = mm(jnp.concatenate(lt3 + l3, 0), jnp.concatenate([b, b, b, tb, tb, tb], 0), TN)
    for h in range(q_s.shape[0]):
        cols = slice(h * HS, (h + 1) * HS)
        q_s[h] = q_all[:, cols].astype(bf16)
        t_s[h] = t_all[:, cols].astype(bf16)
        g_s[h] = cot_ref[:, cols]


def pick(ref, ti):
    v = ref[pl.ds(ti * TILE, TILE)]
    return v.reshape(TILE * v.shape[1], HS)


def weights(s, mc, kblk, vblk, t2, g2):
    e = jnp.exp2(s * CEXP - mc)
    t = mm(kblk, t2, NT)
    p = mm(vblk, g2, NT)
    w1 = e * p
    w2 = e * t
    w3 = w1 * t
    return jnp.concatenate([e.astype(bf16), w1.astype(bf16), w2.astype(bf16), w3.astype(bf16)], axis=1)


def transpose_keys(kblk):
    return jnp.concatenate([kblk.T, jnp.ones((ONES, kblk.shape[0]), bf16)], axis=0)


def own_tile(ti, first, base, starts, kblk, vblk, kt, q_s, t_s, g_s, s_own, acc_o, m_o):
    rows = starts.shape[1]
    n_keys = kblk.shape[0]
    lead = pl.ds(0, n_keys)
    pos = base + lax.broadcasted_iota(jnp.int32, (1, rows), 1)
    starts2 = jnp.concatenate([starts] * TILE, axis=1)
    pos2 = jnp.concatenate([pos] * TILE, axis=1)
    s = mm(kblk[...], pick(q_s, ti), NT)
    kp = first + lax.broadcasted_iota(jnp.int32, s.shape, 0)
    s = jnp.where((kp >= starts2) & (kp <= pos2), s, -1e30)
    s_own[lead, :] = s
    m = jnp.max(jnp.max(s.reshape(n_keys // 8, 8, s.shape[1]), axis=0), axis=0, keepdims=True)
    m_o[ti] = jnp.broadcast_to(m, m_o.shape[1:])
    w = weights(s_own[lead, :], m * CEXP, kblk[...], vblk[...], pick(t_s, ti), pick(g_s, ti))
    acc_o[ti] = mm(kt[:, lead], w)


def prev_tile(ti, first, starts, kblk, vblk, kt, q_s, t_s, g_s, s_own, acc_i, acc_o, m_i, m_o):
    n_keys = kblk.shape[0]
    starts2 = jnp.concatenate([starts] * TILE, axis=1)
    s = mm(kblk[...], pick(q_s, ti), NT)
    kp = first + lax.broadcasted_iota(jnp.int32, s.shape, 0)
    s = jnp.where(kp >= starts2, s, -1e30)
    s_own[...] = s
    m_old = m_i[ti][0:1]
    m = jnp.max(jnp.max(s.reshape(n_keys // 8, 8, s.shape[1]), axis=0), axis=0, keepdims=True)
    mc = jnp.maximum(m_old, m) * CEXP
    if m_o is not None:
        m_o[ti] = jnp.broadcast_to(jnp.maximum(m_old, m), m_o.shape[1:])
    factor = jnp.exp2(m_old * CEXP - mc)
    w = weights(s_own[...], mc, kblk[...], vblk[...], pick(t_s, ti), pick(g_s, ti))
    acc_o[ti] = acc_i[ti] * jnp.concatenate([factor] * 4, axis=1) + mm(kt[...], w)


def attend_kernel(kb_len, own_fn, starts_ref, q_s, t_s, g_s, k_ref, v_ref, m_in, acc_in, m_ref, acc, s_buf, kt, m_new, fac):
    lanes = TILE * starts_ref.shape[1]
    starts = starts_ref[...]
    start_last = jnp.max(starts)
    lo = jnp.min(starts) // kb_len
    hi = own_fn()
    starts2 = jnp.concatenate([starts] * TILE, axis=1)

    def build(kb, c):
        off = pl.multiple_of(kb * kb_len, kb_len)
        kt[:, pl.ds(off, kb_len)] = transpose_keys(k_ref[pl.ds(off, kb_len), :])
        return c

    lax.fori_loop(lo, hi, build, 0)

    def one_tile(ti, carry):
        q2, t2, g2 = pick(q_s, ti), pick(t_s, ti), pick(g_s, ti)
        m_old = m_ref[ti]
        m_new[...] = m_old

        def pass1(kb, c):
            off = pl.multiple_of(kb * kb_len, kb_len)

            def keep(s):
                s_buf[pl.ds(off, kb_len), :] = s
                m_new[...] = jnp.maximum(m_new[...], jnp.max(s.reshape(kb_len // 8, 8, lanes), axis=0))

            @pl.when(off < start_last)
            def _():
                s = mm(k_ref[pl.ds(off, kb_len), :], q2, NT)
                kp = off + lax.broadcasted_iota(jnp.int32, (kb_len, lanes), 0)
                keep(jnp.where(kp >= starts2, s, -1e30))

            @pl.when(off >= start_last)
            def _():
                keep(mm(k_ref[pl.ds(off, kb_len), :], q2, NT))
            return c

        lax.fori_loop(lo, hi, pass1, 0)
        m = jnp.max(m_new[...], axis=0, keepdims=True)
        mc = m * CEXP
        factor = jnp.exp2(m_old[0:1] * CEXP - mc)
        fac[...] = jnp.concatenate([factor] * 4, axis=1)
        m_ref[ti] = jnp.broadcast_to(m, m_new.shape)

        def pass2(kb, c):
            off = pl.multiple_of(kb * kb_len, kb_len)
            w = weights(s_buf[pl.ds(off, kb_len), :], mc, k_ref[pl.ds(off, kb_len), :], v_ref[pl.ds(off, kb_len), :], t2, g2)
            acc[ti] = acc[ti] * fac[...] + mm(kt[:, pl.ds(off, kb_len)], w)
            fac[...] = jnp.ones_like(fac)
            return c

        lax.fori_loop(lo, hi, pass2, 0)
        return carry

    lax.fori_loop(0, jnp.where(lo < hi, acc.shape[0], 0), one_tile, 0)


def attend(starts, m_o, q_s, t_s, g_s, k, v, acc, own_fn, kb_len):
    total = k.shape[0]
    lanes = TILE * starts.shape[1]
    vm = pl.BlockSpec(memory_space=pltpu.VMEM)
    return pl.pallas_call(
        functools.partial(attend_kernel, kb_len, own_fn),
        out_shape=(jax.ShapeDtypeStruct(m_o.shape, f32), jax.ShapeDtypeStruct(acc.shape, f32)),
        in_specs=[vm] * 8,
        out_specs=(vm, vm),
        scratch_shapes=[
            pltpu.VMEM((total, lanes), f32),
            pltpu.VMEM((HS + ONES, total), bf16),
            pltpu.VMEM((8, lanes), f32),
            pltpu.VMEM((1, 4 * lanes), f32),
        ],
        input_output_aliases={6: 0, 7: 1},
        compiler_params=pltpu.CompilerParams(vmem_limit_bytes=32 << 20),
        name="attend",
    )(starts, q_s, t_s, g_s, k, v, m_o, acc)


def close_tiles(acc_ref, accs, low_t, b, tb, zp, bp):
    rows = low_t.shape[1]
    lanes = TILE * rows
    l3 = split2(low_t[0:16, :])
    lt3 = split2(low_t[16:32, :])
    llt = jnp.concatenate([lt3[0], lt3[0], lt3[1], l3[0], l3[0], l3[1]], axis=1)
    zz = jnp.zeros((16, rows), f32)
    for ti in range(acc_ref.shape[0]):
        a = acc_ref[ti] if ti < LATE else accs[ti - LATE]
        k0, k1, k2, k3 = (a[0:HS, n * lanes:(n + 1) * lanes] for n in range(4))
        l, aa, bb, cc = (a[HS:HS + 1, n * lanes:(n + 1) * lanes] for n in range(4))
        inv = 1.0 / l
        delta = aa * inv
        mt = bb * inv * SCALE
        dd = cc * inv * SCALE - mt * delta
        f = SCALE * inv
        grad = (k1 - delta * k0) * f
        gdot = (SCALE * (k3 - delta * k2) - mt * k1 + (mt * delta - dd) * k0) * f
        gh, gl = split2(grad)
        dh, dl = split2(gdot)
        for j in range(TILE):
            cols = slice((ti * TILE + j) * HS, (ti * TILE + j + 1) * HS)
            bj, tbj = b[:, cols], tb[:, cols]
            ln = slice(j * rows, (j + 1) * rows)
            zz += mm(jnp.concatenate([bj, bj, tbj, tbj], 1),
                     jnp.concatenate([dh[:, ln], dl[:, ln], gh[:, ln], gl[:, ln]], 0))
            r = jnp.concatenate([gh[:, ln], gl[:, ln], gh[:, ln], dh[:, ln], dl[:, ln], dh[:, ln]], axis=1)
            bp[ti * TILE + j] = mm(llt, r, NT)
    zp[...] = zz


from jax.sharding import PartitionSpec as P

MESH = pl.DeviceIdType.MESH
LATE = 3


class Shifted:
    def __init__(self, ref, by):
        self.ref, self.by = ref, by

    def __setitem__(self, i, v):
        self.ref[i - self.by] = v

NX, NC, NZ = 4, 2, 4
GROUP = NX * NC


def place():
    ctx = lax.axis_index("ctx")
    return ctx, ctx // GROUP, (ctx // NC) % NX, ctx % NC


def at(z, x, core):
    return (z % NZ) * GROUP + (x % NX) * NC + core


def greet(ctx_peers, head_peers):
    barrier = pltpu.get_barrier_semaphore()
    for p in ctx_peers:
        pl.semaphore_signal(barrier, inc=1, device_id={"ctx": p}, device_id_type=MESH)
    for p in head_peers:
        pl.semaphore_signal(barrier, inc=1, device_id={"head": p}, device_id_type=MESH)
    return lambda: pl.semaphore_wait(barrier, len(ctx_peers) + len(head_peers))


def gather_kernel(n_head, k_ref, v_ref, x_ref, a_ref, ta_ref, qb_ref, cot_ref, b_ref, tb_ref, seg_ref, docs_ref,
                  kall, vall, low_ref, x_o, b_o, tb_o, starts_ref, q_s, t_s, g_s, acc_o, m_o,
                  qb_o, cot_o, s_own, kt, a_s, parts, mine, seg_s, docs_s, rk, rv, rl, ss, sl, loc):
    ctx, z, x, core = place()
    head = lax.axis_index("head")
    rows = k_ref.shape[0]
    heads = [lax.rem(head + d, n_head) for d in range(1, n_head)]
    twin = at(z, x, 1 - core)
    sides = [at(z, x + dx, core) for dx in (2, 1, 3)]
    ahead = [at(z + dz, x, core) for dz in range(NZ)]
    ready = greet(sides + [ahead[1], ahead[3], twin], heads)

    def cut(ref, j):
        return ref.at[pl.ds(pl.multiple_of(j * rows, rows), rows), :]

    pairs = [(x_ref, x_o), (a_ref, a_s.at[0:16]), (ta_ref, a_s.at[16:32]), (k_ref, cut(kall, ctx)), (v_ref, cut(vall, ctx)),
             (seg_ref, seg_s), (docs_ref, docs_s), (qb_ref, qb_o), (cot_ref, cot_o), (b_ref, b_o), (tb_ref, tb_o)]
    loads = [pltpu.make_async_copy(s, d, loc.at[i]) for i, (s, d) in enumerate(pairs)]
    for c in loads:
        c.start()
    for c in loads[:3]:
        c.wait()
    part = mm(a_s[...], x_o[...], NT)
    mine[...] = part
    parts[pl.ds(head, 1)] = part[None]
    ready()
    lows = []
    for i, p in enumerate(heads):
        c = pltpu.make_async_remote_copy(
            src_ref=mine, dst_ref=parts.at[head], send_sem=sl.at[i], recv_sem=rl.at[head],
            device_id={"head": p}, device_id_type=MESH)
        c.start()
        lows.append(c)

    sends = []
    count = [0]

    def push(kv, j, tos, cond=None, src=None):
        ref, sem = kv
        for to in tos:
            n = count[0]
            count[0] += 1

            def make(n=n, to=to):
                return pltpu.make_async_remote_copy(
                    src_ref=cut(ref, j) if src is None else src, dst_ref=cut(ref, j), send_sem=ss.at[n],
                    recv_sem=sem.at[j], device_id={"ctx": to}, device_id_type=MESH)

            make().start()
            sends.append((cond, make))

    K, V = (kall, rk), (vall, rv)

    def arrive(kv, j):
        ref, sem = kv
        pltpu.make_async_remote_copy(
            src_ref=cut(ref, j), dst_ref=cut(ref, j), send_sem=ss.at[0], recv_sem=sem.at[j],
            device_id={"ctx": twin}, device_id_type=MESH).wait_recv()

    def when(cond, f):
        if cond is None:
            f()
        else:
            pl.when(cond)(f)

    has = {0: None, 1: z >= 1, 2: z >= 2, 3: z >= 3}
    to1, to3, both = z <= 2, z == 0, (z >= 1) & (z <= 2)
    spot = [[at(z + NZ - d, x + dx, core) for dx in range(NX)] for d in range(NZ)]
    other = [[at(z + NZ - d, xx, 1 - core) for xx in range(NX)] for d in range(NZ)]

    for kv, src in ((K, k_ref), (V, v_ref)):
        when(to1, lambda: push(kv, ctx, [ahead[1]], to1, src))
        push(kv, ctx, sides + [twin], None, src)
    for kv, src in ((K, k_ref), (V, v_ref)):
        when(to3, lambda: push(kv, ctx, [ahead[3]], to3, src))

    for c in loads[3:]:
        c.wait()
    seg = seg_s[...]
    starts = jnp.zeros(seg.shape, jnp.int32)
    for d in range(docs_s.shape[0]):
        starts = jnp.where(seg == d, docs_s[d], starts)
    starts_ref[...] = starts

    def row(d):
        for kv in (K, V):
            for dx in (1, 3, 2):
                arrive(kv, spot[d][dx])
                push(kv, spot[d][dx], [twin], has[d])

    def column(d, part=(0, 1)):
        for kv in [(K, V)[i] for i in part]:
            arrive(kv, spot[d][0])
            if d == 1:
                when(both, lambda: push(kv, spot[d][0], [ahead[1]], both))
            push(kv, spot[d][0], sides + [twin], has[d])

    def low_sum():
        for i, p in enumerate(heads):
            pltpu.make_async_remote_copy(
                src_ref=mine, dst_ref=parts.at[p], send_sem=sl.at[i], recv_sem=rl.at[p],
                device_id={"head": p}, device_id_type=MESH).wait_recv()
        low_ref[...] = jnp.sum(parts[...], axis=0)

    def twins(d):
        for xx in range(NX):
            j = other[d][xx]
            arrive(K, j)
            arrive(V, j)

    when(has[1], lambda: column(1))
    when(has[3], lambda: column(3))
    row(0)
    low_sum()
    make_queries(low_ref[...], qb_o, cot_o, b_o[...], tb_o[...], q_s, t_s, g_s)
    twins(0)
    span = GROUP * rows
    first = pl.multiple_of(z * span, span)
    kblk, vblk = kall.at[pl.ds(first, span), :], vall.at[pl.ds(first, span), :]
    kt[...] = transpose_keys(kblk[...])

    u = lax.rem(ctx, GROUP)

    def own(ti):
        for low_u, high_u in ((0, 4), (4, 6), (6, 8)):
            @pl.when((u >= low_u) & (u < high_u))
            def _():
                n = high_u * rows
                kb, vb = kall.at[pl.ds(first, n), :], vall.at[pl.ds(first, n), :]
                own_tile(ti, first, ctx * rows, starts, kb, vb, kt, q_s, t_s, g_s, s_own, acc_o, m_o)

    own(0)
    own(1)
    when(has[2], lambda: column(2))
    own(2)
    when(has[1], lambda: row(1))
    own(3)
    when(has[1], lambda: twins(1))
    back = pl.multiple_of(jnp.maximum(z - 1, 0) * span, span)
    kpre, vpre = kall.at[pl.ds(back, span), :], vall.at[pl.ds(back, span), :]

    def older(lo, hi):
        for ti in range(lo, hi):
            prev_tile(ti, back, starts, kpre, vpre, kt, q_s, t_s, g_s, s_own, acc_o, acc_o, m_o, m_o)

    def older_first():
        kt[...] = transpose_keys(kpre[...])
        older(0, 2)

    when(has[1], older_first)
    when(has[2], lambda: row(2))
    when(has[3], lambda: row(3))
    when(has[1], lambda: older(2, LATE))
    for d in range(2, NZ):
        when(has[d], lambda: twins(d))
    groups = {}
    for cond, make in sends:
        groups.setdefault(id(cond), (cond, []))[1].append(make)

    def drain(makes):
        for make in makes:
            make().wait_send()

    for cond, makes in groups.values():
        when(cond, lambda: drain(makes))
    for c in lows:
        c.wait_send()


def gather(k, v, x, a_t, ta_t, qb, cot, b, tb, seg, docs, n_ctx, n_head):
    rows, width = k.shape
    vm = pl.BlockSpec(memory_space=pltpu.VMEM)
    hb = pl.BlockSpec(memory_space=pltpu.HBM)
    dma = pltpu.SemaphoreType.DMA
    like = jax.ShapeDtypeStruct
    args = (k, v, x, a_t, ta_t, qb, cot, b, tb, seg.reshape(1, rows), docs)
    n_q = qb.shape[1] // HS
    stack = like((n_q, rows, HS), bf16)
    lanes = TILE * rows
    return pl.pallas_call(
        functools.partial(gather_kernel, n_head),
        out_shape=(like((n_ctx * rows, width), bf16), like((n_ctx * rows, width), bf16), like((32, rows), f32),
                   like(x.shape, bf16), like(b.shape, bf16), like(tb.shape, bf16), like((1, rows), jnp.int32),
                   stack, stack, stack, like((n_q // TILE, HS + ONES, 4 * lanes), f32), like((n_q // TILE, 8, lanes), f32)),
        in_specs=[hb] * 11,
        out_specs=(vm,) * 12,
        scratch_shapes=[
            pltpu.VMEM(qb.shape, bf16),
            pltpu.VMEM(cot.shape, bf16),
            pltpu.VMEM((GROUP * rows, lanes), f32),
            pltpu.VMEM((HS + ONES, GROUP * rows), bf16),
            pltpu.VMEM((32, x.shape[1]), bf16),
            pltpu.VMEM((n_head, 32, rows), f32),
            pltpu.VMEM((32, rows), f32),
            pltpu.VMEM((1, rows), jnp.int32),
            pltpu.SMEM(docs.shape, jnp.int32),
            dma((n_ctx,)), dma((n_ctx,)), dma((n_head,)), dma((96,)), dma((n_head,)), dma((11,)),
        ],
        compiler_params=pltpu.CompilerParams(collective_id=0, has_side_effects=True, vmem_limit_bytes=20 << 20),
        name="gather",
    )(*(pltpu.with_memory_space_constraint(r, pltpu.HBM) for r in args))


def reduce_kernel(n_head, acc_ref, m_ref, starts_ref, kall, vall, q_s, t_s, g_s, low_ref, b_ref, tb_ref, x_ref, oa_ref, ob_ref,
                  accs, kt, s_own, zp_ref, zbuf, sa, sb, ra, rb, ca, cb, ta, tb,
                  rz, zs, rsa, rsb, ssa, ssb, rca, rcb, sca, scb, rga, rgb, sga, sgb):
    ctx, z, x, core = place()
    u = lax.rem(ctx, GROUP)
    head = lax.axis_index("head")
    heads = [lax.rem(head // 4 + dl, 2) * 4 + lax.rem(head + dy, 4)
             for dl, dy in ((1, 2), (1, 1), (1, 3), (0, 2), (1, 0), (0, 1), (0, 3))]
    mates = [lax.rem(u // 2 + dx, NX) * 2 + lax.rem(u + dc, 2)
             for dx, dc in ((2, 1), (2, 0), (1, 1), (3, 1), (1, 0), (3, 0), (0, 1))]
    cols = [lax.rem(z + d, NZ) for d in (2, 1, 3)]
    ready = greet([z * GROUP + m for m in mates] + [c * GROUP + u for c in cols], heads)
    accs[...] = acc_ref[LATE:]

    @pl.when(z >= 1)
    def _():
        span = GROUP * x_ref.shape[0]
        back = pl.multiple_of(jnp.maximum(z - 1, 0) * span, span)
        kpre, vpre = kall.at[pl.ds(back, span), :], vall.at[pl.ds(back, span), :]
        kt[...] = transpose_keys(kpre[...])
        for ti in range(LATE, acc_ref.shape[0]):
            prev_tile(ti, back, starts_ref[...], kpre, vpre, kt, q_s, t_s, g_s, s_own, acc_ref,
                      Shifted(accs, LATE), m_ref, None)

    close_tiles(acc_ref, accs, low_ref[...], b_ref[...], tb_ref[...], zp_ref, sb)
    zbuf[pl.ds(head, 1)] = zp_ref[...][None]
    ready()
    sends = []

    def copy(src, dst, ssem, rsem, dev):
        return pltpu.make_async_remote_copy(src_ref=src, dst_ref=dst, send_sem=ssem, recv_sem=rsem,
                                            device_id=dev, device_id_type=MESH)

    def start(c):
        c.start()
        sends.append(c)

    for i, p in enumerate(heads):
        start(copy(zp_ref, zbuf.at[head], zs.at[i], rz.at[head], {"head": p}))

    def scatter(s, r, ssem, rsem):
        for i, m in enumerate(mates):
            start(copy(s.at[m], r.at[u], ssem.at[i], rsem.at[u], {"ctx": z * GROUP + m}))
        r[pl.ds(u, 1)] = s[pl.ds(u, 1)]

    def across(r, c, s, rsem, ssem2, rsem2):
        for i, m in enumerate(mates):
            copy(r.at[m], r.at[m], ssem2.at[0], rsem.at[m], {"ctx": z * GROUP + m}).wait_recv()
        part = jnp.sum(r[...], axis=0)
        s[...] = part
        c[pl.ds(z, 1)] = part[None]
        for i, q in enumerate(cols):
            start(copy(s, c.at[z], ssem2.at[i], rsem2.at[z], {"ctx": q * GROUP + u}))

    def spread(c, t, o, ssem, rsem, ssem2, rsem2):
        for i, q in enumerate(cols):
            copy(t.at[q], c.at[q], ssem.at[0], rsem.at[q], {"ctx": q * GROUP + u}).wait_recv()
        t[pl.ds(u, 1)] = jnp.sum(c[...], axis=0)[None]
        for i, m in enumerate(mates):
            start(copy(t.at[u], t.at[u], ssem2.at[i], rsem2.at[u], {"ctx": z * GROUP + m}))

    def collect(t, o, ssem, rsem):
        for m in mates:
            copy(t.at[m], t.at[m], ssem.at[0], rsem.at[m], {"ctx": z * GROUP + m}).wait_recv()
        for i in range(GROUP):
            o[:, i * HS:(i + 1) * HS] = t[i]

    scatter(sb, rb, ssb, rsb)
    for i, p in enumerate(heads):
        copy(zp_ref, zbuf.at[p], zs.at[0], rz.at[p], {"head": p}).wait_recv()
    zsum = jnp.sum(zbuf[...], axis=0)
    z3 = jnp.concatenate(split3(zsum), 0)
    for i in range(0, GROUP, 2):
        ap = mm(z3, x_ref[:, i * HS:(i + 2) * HS])
        ap = ap[0:16] + ap[16:32] + ap[32:48]
        sa[i] = ap[:, :HS]
        sa[i + 1] = ap[:, HS:]
    scatter(sa, ra, ssa, rsa)
    across(rb, cb, sb_part(sb), rsb, scb, rcb)
    across(ra, ca, sb_part(sa), rsa, sca, rca)
    spread(cb, tb, ob_ref, scb, rcb, sgb, rgb)
    spread(ca, ta, oa_ref, sca, rca, sga, rga)
    collect(tb, ob_ref, sgb, rgb)
    collect(ta, oa_ref, sga, rga)
    for c in sends:
        c.wait_send()


def sb_part(s):
    return s.at[GROUP]


def reduce(acc, m_o, starts, kall, vall, q_s, t_s, g_s, low_t, b, tb, x, n_head):
    width = b.shape[1]
    rows = low_t.shape[1]
    vm = pl.BlockSpec(memory_space=pltpu.VMEM)
    out = jax.ShapeDtypeStruct((16, width), f32)
    dma = pltpu.SemaphoreType.DMA
    return pl.pallas_call(
        functools.partial(reduce_kernel, n_head),
        out_shape=(out, out),
        in_specs=[vm] * 12,
        out_specs=(vm, vm),
        scratch_shapes=[
            pltpu.VMEM((acc.shape[0] - LATE,) + acc.shape[1:], f32),
            pltpu.VMEM((HS + ONES, GROUP * rows), bf16),
            pltpu.VMEM((GROUP * rows, TILE * rows), f32),
            pltpu.VMEM((16, rows), f32),
            pltpu.VMEM((n_head, 16, rows), f32),
            pltpu.VMEM((GROUP + 1, 16, HS), f32), pltpu.VMEM((GROUP + 1, 16, HS), f32),
            pltpu.VMEM((GROUP, 16, HS), f32), pltpu.VMEM((GROUP, 16, HS), f32),
            pltpu.VMEM((NZ, 16, HS), f32), pltpu.VMEM((NZ, 16, HS), f32),
            pltpu.VMEM((GROUP, 16, HS), f32), pltpu.VMEM((GROUP, 16, HS), f32),
            dma((n_head,)), dma((n_head,)),
            dma((GROUP,)), dma((GROUP,)), dma((GROUP,)), dma((GROUP,)),
            dma((NZ,)), dma((NZ,)), dma((NZ,)), dma((NZ,)),
            dma((GROUP,)), dma((GROUP,)), dma((GROUP,)), dma((GROUP,)),
        ],
        compiler_params=pltpu.CompilerParams(collective_id=1, has_side_effects=True, vmem_limit_bytes=12 << 20),
        name="reduce",
    )(acc, m_o, starts, kall, vall, q_s, t_s, g_s, low_t, b, tb, x)


def finish_kernel(a_ref, b_ref, oa_ref, ob_ref, sem):
    copies = [pltpu.make_async_copy(a_ref, oa_ref, sem.at[0]), pltpu.make_async_copy(b_ref, ob_ref, sem.at[1])]
    for c in copies:
        c.start()
    for c in copies:
        c.wait()


def finish(a, b):
    vm = pl.BlockSpec(memory_space=pltpu.VMEM)
    hb = pl.BlockSpec(memory_space=pltpu.HBM)
    return pl.pallas_call(
        finish_kernel,
        out_shape=(jax.ShapeDtypeStruct(a.shape, f32), jax.ShapeDtypeStruct(b.shape, f32)),
        in_specs=[vm, vm],
        out_specs=(hb, hb),
        scratch_shapes=[pltpu.SemaphoreType.DMA((2,))],
        compiler_params=pltpu.CompilerParams(vmem_limit_bytes=1 << 20),
        name="finish",
    )(a, b)


def on_device(n_ctx, n_head, activations, query_base, key_rows, values, out_cotangent, adapter_a, adapter_b, tangent_a, tangent_b,
              segment_ids, doc_starts):
    rows = activations.shape[0]
    kall, vall, low_t, x, b, tb, starts, q_s, t_s, g_s, acc, m_o = gather(
        key_rows, values, activations, adapter_a.T, tangent_a.T, query_base, out_cotangent, adapter_b, tangent_b,
        segment_ids, doc_starts, n_ctx, n_head)
    m_o, acc = attend(starts, m_o, q_s, t_s, g_s, kall, vall, acc, lambda: jnp.maximum(lax.axis_index("ctx") // GROUP - 1, 0), GROUP * rows)
    oa, ob = finish(*reduce(acc, m_o, starts, kall, vall, q_s, t_s, g_s, low_t, b, tb, x, n_head))
    return oa.T, ob


def solution(mesh):
    wide = P("ctx", "head")
    placed = (wide,) * 5 + (P("head", None), P(None, "head"), P("head", None), P(None, "head"), P("ctx"), P())
    return jax.shard_map(
        functools.partial(on_device, mesh.shape["ctx"], mesh.shape["head"]),
        mesh=mesh,
        in_specs=placed,
        out_specs=(P("head", None), P(None, "head")),
        check_vma=False,
    )
```

```python
import functools, math
import jax, jax.numpy as jnp
from jax import lax
from jax.experimental import pallas as pl
from jax.experimental.pallas import tpu as pltpu

HS = 128
TILE = 2
ONES = 16
NT = (((1,), (1,)), ((), ()))
TN = (((0,), (0,)), ((), ()))
NN = (((1,), (0,)), ((), ()))
f32, bf16 = jnp.float32, jnp.bfloat16
SCALE = 1.0 / math.sqrt(HS)
CEXP = SCALE * math.log2(math.e)


def mm(a, b, dims=NN):
    return lax.dot_general(a, b, dims, preferred_element_type=f32)


def split2(x):
    hi = x.astype(bf16)
    return hi, (x - hi.astype(f32)).astype(bf16)


def split3(x):
    hi = x.astype(bf16)
    r = x - hi.astype(f32)
    mid = r.astype(bf16)
    return hi, mid, (r - mid.astype(f32)).astype(bf16)


def make_queries(low_t, qb_ref, cot_ref, b, tb, q_s, t_s, g_s):
    l3 = split3(low_t[0:16, :])
    lt3 = split3(low_t[16:32, :])
    q_all = mm(jnp.concatenate(l3, 0), jnp.concatenate([b, b, b], 0), TN) + qb_ref[...].astype(f32)
    t_all = mm(jnp.concatenate(lt3 + l3, 0), jnp.concatenate([b, b, b, tb, tb, tb], 0), TN)
    for h in range(q_s.shape[0]):
        cols = slice(h * HS, (h + 1) * HS)
        q_s[h] = q_all[:, cols].astype(bf16)
        t_s[h] = t_all[:, cols].astype(bf16)
        g_s[h] = cot_ref[:, cols]


def pick(ref, ti):
    v = ref[pl.ds(ti * TILE, TILE)]
    return v.reshape(TILE * v.shape[1], HS)


def weights(s, mc, kblk, vblk, t2, g2):
    e = jnp.exp2(s * CEXP - mc)
    t = mm(kblk, t2, NT)
    p = mm(vblk, g2, NT)
    w1 = e * p
    w2 = e * t
    w3 = w1 * t
    return jnp.concatenate([e.astype(bf16), w1.astype(bf16), w2.astype(bf16), w3.astype(bf16)], axis=1)


def transpose_keys(kblk):
    return jnp.concatenate([kblk.T, jnp.ones((ONES, kblk.shape[0]), bf16)], axis=0)


def own_tile(ti, first, base, starts, kblk, vblk, kt, q_s, t_s, g_s, s_own, acc_o, m_o):
    rows = starts.shape[1]
    n_keys = kblk.shape[0]
    lead = pl.ds(0, n_keys)
    pos = base + lax.broadcasted_iota(jnp.int32, (1, rows), 1)
    starts2 = jnp.concatenate([starts] * TILE, axis=1)
    pos2 = jnp.concatenate([pos] * TILE, axis=1)
    s = mm(kblk[...], pick(q_s, ti), NT)
    kp = first + lax.broadcasted_iota(jnp.int32, s.shape, 0)
    s = jnp.where((kp >= starts2) & (kp <= pos2), s, -1e30)
    s_own[lead, :] = s
    m = jnp.max(jnp.max(s.reshape(n_keys // 8, 8, s.shape[1]), axis=0), axis=0, keepdims=True)
    m_o[ti] = jnp.broadcast_to(m, m_o.shape[1:])
    w = weights(s_own[lead, :], m * CEXP, kblk[...], vblk[...], pick(t_s, ti), pick(g_s, ti))
    acc_o[ti] = mm(kt[:, lead], w)


def prev_tile(ti, first, starts, kblk, vblk, kt, q_s, t_s, g_s, s_own, acc_i, acc_o, m_i, m_o):
    n_keys = kblk.shape[0]
    starts2 = jnp.concatenate([starts] * TILE, axis=1)
    s = mm(kblk[...], pick(q_s, ti), NT)
    kp = first + lax.broadcasted_iota(jnp.int32, s.shape, 0)
    s = jnp.where(kp >= starts2, s, -1e30)
    s_own[...] = s
    m_old = m_i[ti][0:1]
    m = jnp.max(jnp.max(s.reshape(n_keys // 8, 8, s.shape[1]), axis=0), axis=0, keepdims=True)
    mc = jnp.maximum(m_old, m) * CEXP
    if m_o is not None:
        m_o[ti] = jnp.broadcast_to(jnp.maximum(m_old, m), m_o.shape[1:])
    factor = jnp.exp2(m_old * CEXP - mc)
    w = weights(s_own[...], mc, kblk[...], vblk[...], pick(t_s, ti), pick(g_s, ti))
    acc_o[ti] = acc_i[ti] * jnp.concatenate([factor] * 4, axis=1) + mm(kt[...], w)


def attend_kernel(kb_len, own_fn, starts_ref, q_s, t_s, g_s, k_ref, v_ref, m_in, acc_in, m_ref, acc, s_buf, kt, m_new, fac):
    lanes = TILE * starts_ref.shape[1]
    starts = starts_ref[...]
    start_last = jnp.max(starts)
    lo = jnp.min(starts) // kb_len
    hi = own_fn()
    starts2 = jnp.concatenate([starts] * TILE, axis=1)

    def build(kb, c):
        off = pl.multiple_of(kb * kb_len, kb_len)
        kt[:, pl.ds(off, kb_len)] = transpose_keys(k_ref[pl.ds(off, kb_len), :])
        return c

    lax.fori_loop(lo, hi, build, 0)

    def one_tile(ti, carry):
        q2, t2, g2 = pick(q_s, ti), pick(t_s, ti), pick(g_s, ti)
        m_old = m_ref[ti]
        m_new[...] = m_old

        def pass1(kb, c):
            off = pl.multiple_of(kb * kb_len, kb_len)

            def keep(s):
                s_buf[pl.ds(off, kb_len), :] = s
                m_new[...] = jnp.maximum(m_new[...], jnp.max(s.reshape(kb_len // 8, 8, lanes), axis=0))

            @pl.when(off < start_last)
            def _():
                s = mm(k_ref[pl.ds(off, kb_len), :], q2, NT)
                kp = off + lax.broadcasted_iota(jnp.int32, (kb_len, lanes), 0)
                keep(jnp.where(kp >= starts2, s, -1e30))

            @pl.when(off >= start_last)
            def _():
                keep(mm(k_ref[pl.ds(off, kb_len), :], q2, NT))
            return c

        lax.fori_loop(lo, hi, pass1, 0)
        m = jnp.max(m_new[...], axis=0, keepdims=True)
        mc = m * CEXP
        factor = jnp.exp2(m_old[0:1] * CEXP - mc)
        fac[...] = jnp.concatenate([factor] * 4, axis=1)
        m_ref[ti] = jnp.broadcast_to(m, m_new.shape)

        def pass2(kb, c):
            off = pl.multiple_of(kb * kb_len, kb_len)
            w = weights(s_buf[pl.ds(off, kb_len), :], mc, k_ref[pl.ds(off, kb_len), :], v_ref[pl.ds(off, kb_len), :], t2, g2)
            acc[ti] = acc[ti] * fac[...] + mm(kt[:, pl.ds(off, kb_len)], w)
            fac[...] = jnp.ones_like(fac)
            return c

        lax.fori_loop(lo, hi, pass2, 0)
        return carry

    lax.fori_loop(0, jnp.where(lo < hi, acc.shape[0], 0), one_tile, 0)


def attend(starts, m_o, q_s, t_s, g_s, k, v, acc, own_fn, kb_len):
    total = k.shape[0]
    lanes = TILE * starts.shape[1]
    vm = pl.BlockSpec(memory_space=pltpu.VMEM)
    return pl.pallas_call(
        functools.partial(attend_kernel, kb_len, own_fn),
        out_shape=(jax.ShapeDtypeStruct(m_o.shape, f32), jax.ShapeDtypeStruct(acc.shape, f32)),
        in_specs=[vm] * 8,
        out_specs=(vm, vm),
        scratch_shapes=[
            pltpu.VMEM((total, lanes), f32),
            pltpu.VMEM((HS + ONES, total), bf16),
            pltpu.VMEM((8, lanes), f32),
            pltpu.VMEM((1, 4 * lanes), f32),
        ],
        input_output_aliases={6: 0, 7: 1},
        compiler_params=pltpu.CompilerParams(vmem_limit_bytes=32 << 20),
        name="attend",
    )(starts, q_s, t_s, g_s, k, v, m_o, acc)


def close_tiles(acc_ref, accs, low_t, b, tb, zp, bp):
    rows = low_t.shape[1]
    lanes = TILE * rows
    l3 = split2(low_t[0:16, :])
    lt3 = split2(low_t[16:32, :])
    llt = jnp.concatenate([lt3[0], lt3[0], lt3[1], l3[0], l3[0], l3[1]], axis=1)
    zz = jnp.zeros((16, rows), f32)
    for ti in range(acc_ref.shape[0]):
        a = acc_ref[ti] if ti < LATE else accs[ti - LATE]
        k0, k1, k2, k3 = (a[0:HS, n * lanes:(n + 1) * lanes] for n in range(4))
        l, aa, bb, cc = (a[HS:HS + 1, n * lanes:(n + 1) * lanes] for n in range(4))
        inv = 1.0 / l
        delta = aa * inv
        mt = bb * inv * SCALE
        dd = cc * inv * SCALE - mt * delta
        f = SCALE * inv
        grad = (k1 - delta * k0) * f
        gdot = (SCALE * (k3 - delta * k2) - mt * k1 + (mt * delta - dd) * k0) * f
        gh, gl = split2(grad)
        dh, dl = split2(gdot)
        for j in range(TILE):
            cols = slice((ti * TILE + j) * HS, (ti * TILE + j + 1) * HS)
            bj, tbj = b[:, cols], tb[:, cols]
            ln = slice(j * rows, (j + 1) * rows)
            zz += mm(jnp.concatenate([bj, bj, tbj, tbj], 1),
                     jnp.concatenate([dh[:, ln], dl[:, ln], gh[:, ln], gl[:, ln]], 0))
            r = jnp.concatenate([gh[:, ln], gl[:, ln], gh[:, ln], dh[:, ln], dl[:, ln], dh[:, ln]], axis=1)
            bp[ti * TILE + j] = mm(llt, r, NT)
    zp[...] = zz


from jax.sharding import PartitionSpec as P

MESH = pl.DeviceIdType.MESH
LATE = 3


class Shifted:
    def __init__(self, ref, by):
        self.ref, self.by = ref, by

    def __setitem__(self, i, v):
        self.ref[i - self.by] = v

NX, NC, NZ = 4, 2, 4
GROUP = NX * NC


def place():
    ctx = lax.axis_index("ctx")
    return ctx, ctx // GROUP, (ctx // NC) % NX, ctx % NC


def at(z, x, core):
    return (z % NZ) * GROUP + (x % NX) * NC + core


def greet(ctx_peers, head_peers):
    barrier = pltpu.get_barrier_semaphore()
    for p in ctx_peers:
        pl.semaphore_signal(barrier, inc=1, device_id={"ctx": p}, device_id_type=MESH)
    for p in head_peers:
        pl.semaphore_signal(barrier, inc=1, device_id={"head": p}, device_id_type=MESH)
    return lambda: pl.semaphore_wait(barrier, len(ctx_peers) + len(head_peers))


def gather_kernel(n_head, k_ref, v_ref, x_ref, a_ref, ta_ref, qb_ref, cot_ref, b_ref, tb_ref, seg_ref, docs_ref,
                  kall, vall, low_ref, x_o, b_o, tb_o, starts_ref, q_s, t_s, g_s, acc_o, m_o,
                  qb_o, cot_o, s_own, kt, a_s, parts, mine, seg_s, docs_s, rk, rv, rl, ss, sl, loc):
    ctx, z, x, core = place()
    head = lax.axis_index("head")
    rows = k_ref.shape[0]
    heads = [lax.rem(head + d, n_head) for d in range(1, n_head)]
    twin = at(z, x, 1 - core)
    sides = [at(z, x + dx, core) for dx in (2, 1, 3)]
    ahead = [at(z + dz, x, core) for dz in range(NZ)]
    ready = greet(sides + [ahead[1], ahead[3], twin], heads)

    def cut(ref, j):
        return ref.at[pl.ds(pl.multiple_of(j * rows, rows), rows), :]

    pairs = [(x_ref, x_o), (a_ref, a_s.at[0:16]), (ta_ref, a_s.at[16:32]), (k_ref, cut(kall, ctx)), (v_ref, cut(vall, ctx)),
             (seg_ref, seg_s), (docs_ref, docs_s), (qb_ref, qb_o), (cot_ref, cot_o), (b_ref, b_o), (tb_ref, tb_o)]
    loads = [pltpu.make_async_copy(s, d, loc.at[i]) for i, (s, d) in enumerate(pairs)]
    for c in loads:
        c.start()
    for c in loads[:3]:
        c.wait()
    part = mm(a_s[...], x_o[...], NT)
    mine[...] = part
    parts[pl.ds(head, 1)] = part[None]
    ready()
    lows = []
    for i, p in enumerate(heads):
        c = pltpu.make_async_remote_copy(
            src_ref=mine, dst_ref=parts.at[head], send_sem=sl.at[i], recv_sem=rl.at[head],
            device_id={"head": p}, device_id_type=MESH)
        c.start()
        lows.append(c)

    sends = []
    count = [0]

    def push(kv, j, tos, cond=None, src=None):
        ref, sem = kv
        for to in tos:
            n = count[0]
            count[0] += 1

            def make(n=n, to=to):
                return pltpu.make_async_remote_copy(
                    src_ref=cut(ref, j) if src is None else src, dst_ref=cut(ref, j), send_sem=ss.at[n],
                    recv_sem=sem.at[j], device_id={"ctx": to}, device_id_type=MESH)

            make().start()
            sends.append((cond, make))

    K, V = (kall, rk), (vall, rv)

    def arrive(kv, j):
        ref, sem = kv
        pltpu.make_async_remote_copy(
            src_ref=cut(ref, j), dst_ref=cut(ref, j), send_sem=ss.at[0], recv_sem=sem.at[j],
            device_id={"ctx": twin}, device_id_type=MESH).wait_recv()

    def when(cond, f):
        if cond is None:
            f()
        else:
            pl.when(cond)(f)

    has = {0: None, 1: z >= 1, 2: z >= 2, 3: z >= 3}
    to1, to3, both = z <= 2, z == 0, (z >= 1) & (z <= 2)
    spot = [[at(z + NZ - d, x + dx, core) for dx in range(NX)] for d in range(NZ)]
    other = [[at(z + NZ - d, xx, 1 - core) for xx in range(NX)] for d in range(NZ)]

    for kv, src in ((K, k_ref), (V, v_ref)):
        when(to1, lambda: push(kv, ctx, [ahead[1]], to1, src))
        push(kv, ctx, sides + [twin], None, src)
    for kv, src in ((K, k_ref), (V, v_ref)):
        when(to3, lambda: push(kv, ctx, [ahead[3]], to3, src))

    for c in loads[3:]:
        c.wait()
    seg = seg_s[...]
    starts = jnp.zeros(seg.shape, jnp.int32)
    for d in range(docs_s.shape[0]):
        starts = jnp.where(seg == d, docs_s[d], starts)
    starts_ref[...] = starts

    def row(d):
        for kv in (K, V):
            for dx in (1, 3, 2):
                arrive(kv, spot[d][dx])
                push(kv, spot[d][dx], [twin], has[d])

    def column(d, part=(0, 1)):
        for kv in [(K, V)[i] for i in part]:
            arrive(kv, spot[d][0])
            if d == 1:
                when(both, lambda: push(kv, spot[d][0], [ahead[1]], both))
            push(kv, spot[d][0], sides + [twin], has[d])

    def low_sum():
        for i, p in enumerate(heads):
            pltpu.make_async_remote_copy(
                src_ref=mine, dst_ref=parts.at[p], send_sem=sl.at[i], recv_sem=rl.at[p],
                device_id={"head": p}, device_id_type=MESH).wait_recv()
        low_ref[...] = jnp.sum(parts[...], axis=0)

    def twins(d):
        for xx in range(NX):
            j = other[d][xx]
            arrive(K, j)
            arrive(V, j)

    when(has[1], lambda: column(1))
    when(has[3], lambda: column(3))
    row(0)
    low_sum()
    make_queries(low_ref[...], qb_o, cot_o, b_o[...], tb_o[...], q_s, t_s, g_s)
    twins(0)
    span = GROUP * rows
    first = pl.multiple_of(z * span, span)
    kblk, vblk = kall.at[pl.ds(first, span), :], vall.at[pl.ds(first, span), :]
    kt[...] = transpose_keys(kblk[...])

    u = lax.rem(ctx, GROUP)

    def own(ti):
        for low_u, high_u in ((0, 4), (4, 6), (6, 8)):
            @pl.when((u >= low_u) & (u < high_u))
            def _():
                n = high_u * rows
                kb, vb = kall.at[pl.ds(first, n), :], vall.at[pl.ds(first, n), :]
                own_tile(ti, first, ctx * rows, starts, kb, vb, kt, q_s, t_s, g_s, s_own, acc_o, m_o)

    own(0)
    when(has[2], lambda: column(2, (0,)))
    own(1)
    when(has[2], lambda: column(2, (1,)))
    own(2)
    when(has[1], lambda: row(1))
    own(3)
    when(has[1], lambda: twins(1))
    back = pl.multiple_of(jnp.maximum(z - 1, 0) * span, span)
    kpre, vpre = kall.at[pl.ds(back, span), :], vall.at[pl.ds(back, span), :]

    def older(lo, hi):
        for ti in range(lo, hi):
            prev_tile(ti, back, starts, kpre, vpre, kt, q_s, t_s, g_s, s_own, acc_o, acc_o, m_o, m_o)

    def older_first():
        kt[...] = transpose_keys(kpre[...])
        older(0, 2)

    when(has[1], older_first)
    when(has[2], lambda: row(2))
    when(has[3], lambda: row(3))
    when(has[1], lambda: older(2, LATE))
    for d in range(2, NZ):
        when(has[d], lambda: twins(d))
    groups = {}
    for cond, make in sends:
        groups.setdefault(id(cond), (cond, []))[1].append(make)

    def drain(makes):
        for make in makes:
            make().wait_send()

    for cond, makes in groups.values():
        when(cond, lambda: drain(makes))
    for c in lows:
        c.wait_send()


def gather(k, v, x, a_t, ta_t, qb, cot, b, tb, seg, docs, n_ctx, n_head):
    rows, width = k.shape
    vm = pl.BlockSpec(memory_space=pltpu.VMEM)
    hb = pl.BlockSpec(memory_space=pltpu.HBM)
    dma = pltpu.SemaphoreType.DMA
    like = jax.ShapeDtypeStruct
    args = (k, v, x, a_t, ta_t, qb, cot, b, tb, seg.reshape(1, rows), docs)
    n_q = qb.shape[1] // HS
    stack = like((n_q, rows, HS), bf16)
    lanes = TILE * rows
    return pl.pallas_call(
        functools.partial(gather_kernel, n_head),
        out_shape=(like((n_ctx * rows, width), bf16), like((n_ctx * rows, width), bf16), like((32, rows), f32),
                   like(x.shape, bf16), like(b.shape, bf16), like(tb.shape, bf16), like((1, rows), jnp.int32),
                   stack, stack, stack, like((n_q // TILE, HS + ONES, 4 * lanes), f32), like((n_q // TILE, 8, lanes), f32)),
        in_specs=[hb] * 11,
        out_specs=(vm,) * 12,
        scratch_shapes=[
            pltpu.VMEM(qb.shape, bf16),
            pltpu.VMEM(cot.shape, bf16),
            pltpu.VMEM((GROUP * rows, lanes), f32),
            pltpu.VMEM((HS + ONES, GROUP * rows), bf16),
            pltpu.VMEM((32, x.shape[1]), bf16),
            pltpu.VMEM((n_head, 32, rows), f32),
            pltpu.VMEM((32, rows), f32),
            pltpu.VMEM((1, rows), jnp.int32),
            pltpu.SMEM(docs.shape, jnp.int32),
            dma((n_ctx,)), dma((n_ctx,)), dma((n_head,)), dma((96,)), dma((n_head,)), dma((11,)),
        ],
        compiler_params=pltpu.CompilerParams(collective_id=0, has_side_effects=True, vmem_limit_bytes=20 << 20),
        name="gather",
    )(*(pltpu.with_memory_space_constraint(r, pltpu.HBM) for r in args))


def reduce_kernel(n_head, acc_ref, m_ref, starts_ref, kall, vall, q_s, t_s, g_s, low_ref, b_ref, tb_ref, x_ref, oa_ref, ob_ref,
                  accs, kt, s_own, zp_ref, zbuf, sa, sb, ra, rb, ca, cb, ta, tb,
                  rz, zs, rsa, rsb, ssa, ssb, rca, rcb, sca, scb, rga, rgb, sga, sgb):
    ctx, z, x, core = place()
    u = lax.rem(ctx, GROUP)
    head = lax.axis_index("head")
    heads = [lax.rem(head // 4 + dl, 2) * 4 + lax.rem(head + dy, 4)
             for dl, dy in ((1, 2), (1, 1), (1, 3), (0, 2), (1, 0), (0, 1), (0, 3))]
    mates = [lax.rem(u // 2 + dx, NX) * 2 + lax.rem(u + dc, 2)
             for dx, dc in ((2, 1), (2, 0), (1, 1), (3, 1), (1, 0), (3, 0), (0, 1))]
    cols = [lax.rem(z + d, NZ) for d in (2, 1, 3)]
    ready = greet([z * GROUP + m for m in mates] + [c * GROUP + u for c in cols], heads)
    accs[...] = acc_ref[LATE:]

    @pl.when(z >= 1)
    def _():
        span = GROUP * x_ref.shape[0]
        back = pl.multiple_of(jnp.maximum(z - 1, 0) * span, span)
        kpre, vpre = kall.at[pl.ds(back, span), :], vall.at[pl.ds(back, span), :]
        kt[...] = transpose_keys(kpre[...])
        for ti in range(LATE, acc_ref.shape[0]):
            prev_tile(ti, back, starts_ref[...], kpre, vpre, kt, q_s, t_s, g_s, s_own, acc_ref,
                      Shifted(accs, LATE), m_ref, None)

    close_tiles(acc_ref, accs, low_ref[...], b_ref[...], tb_ref[...], zp_ref, sb)
    zbuf[pl.ds(head, 1)] = zp_ref[...][None]
    ready()
    sends = []

    def copy(src, dst, ssem, rsem, dev):
        return pltpu.make_async_remote_copy(src_ref=src, dst_ref=dst, send_sem=ssem, recv_sem=rsem,
                                            device_id=dev, device_id_type=MESH)

    def start(c):
        c.start()
        sends.append(c)

    for i, p in enumerate(heads):
        start(copy(zp_ref, zbuf.at[head], zs.at[i], rz.at[head], {"head": p}))

    def scatter(s, r, ssem, rsem):
        for i, m in enumerate(mates):
            start(copy(s.at[m], r.at[u], ssem.at[i], rsem.at[u], {"ctx": z * GROUP + m}))
        r[pl.ds(u, 1)] = s[pl.ds(u, 1)]

    def across(r, c, s, rsem, ssem2, rsem2):
        for i, m in enumerate(mates):
            copy(r.at[m], r.at[m], ssem2.at[0], rsem.at[m], {"ctx": z * GROUP + m}).wait_recv()
        part = jnp.sum(r[...], axis=0)
        s[...] = part
        c[pl.ds(z, 1)] = part[None]
        for i, q in enumerate(cols):
            start(copy(s, c.at[z], ssem2.at[i], rsem2.at[z], {"ctx": q * GROUP + u}))

    def spread(c, t, o, ssem, rsem, ssem2, rsem2):
        for i, q in enumerate(cols):
            copy(t.at[q], c.at[q], ssem.at[0], rsem.at[q], {"ctx": q * GROUP + u}).wait_recv()
        t[pl.ds(u, 1)] = jnp.sum(c[...], axis=0)[None]
        for i, m in enumerate(mates):
            start(copy(t.at[u], t.at[u], ssem2.at[i], rsem2.at[u], {"ctx": z * GROUP + m}))

    def collect(t, o, ssem, rsem):
        for m in mates:
            copy(t.at[m], t.at[m], ssem.at[0], rsem.at[m], {"ctx": z * GROUP + m}).wait_recv()
        for i in range(GROUP):
            o[:, i * HS:(i + 1) * HS] = t[i]

    scatter(sb, rb, ssb, rsb)
    for i, p in enumerate(heads):
        copy(zp_ref, zbuf.at[p], zs.at[0], rz.at[p], {"head": p}).wait_recv()
    zsum = jnp.sum(zbuf[...], axis=0)
    z3 = jnp.concatenate(split3(zsum), 0)
    for i in range(0, GROUP, 2):
        ap = mm(z3, x_ref[:, i * HS:(i + 2) * HS])
        ap = ap[0:16] + ap[16:32] + ap[32:48]
        sa[i] = ap[:, :HS]
        sa[i + 1] = ap[:, HS:]
    scatter(sa, ra, ssa, rsa)
    across(rb, cb, sb_part(sb), rsb, scb, rcb)
    across(ra, ca, sb_part(sa), rsa, sca, rca)
    spread(cb, tb, ob_ref, scb, rcb, sgb, rgb)
    spread(ca, ta, oa_ref, sca, rca, sga, rga)
    collect(tb, ob_ref, sgb, rgb)
    collect(ta, oa_ref, sga, rga)
    for c in sends:
        c.wait_send()


def sb_part(s):
    return s.at[GROUP]


def reduce(acc, m_o, starts, kall, vall, q_s, t_s, g_s, low_t, b, tb, x, n_head):
    width = b.shape[1]
    rows = low_t.shape[1]
    vm = pl.BlockSpec(memory_space=pltpu.VMEM)
    out = jax.ShapeDtypeStruct((16, width), f32)
    dma = pltpu.SemaphoreType.DMA
    return pl.pallas_call(
        functools.partial(reduce_kernel, n_head),
        out_shape=(out, out),
        in_specs=[vm] * 12,
        out_specs=(vm, vm),
        scratch_shapes=[
            pltpu.VMEM((acc.shape[0] - LATE,) + acc.shape[1:], f32),
            pltpu.VMEM((HS + ONES, GROUP * rows), bf16),
            pltpu.VMEM((GROUP * rows, TILE * rows), f32),
            pltpu.VMEM((16, rows), f32),
            pltpu.VMEM((n_head, 16, rows), f32),
            pltpu.VMEM((GROUP + 1, 16, HS), f32), pltpu.VMEM((GROUP + 1, 16, HS), f32),
            pltpu.VMEM((GROUP, 16, HS), f32), pltpu.VMEM((GROUP, 16, HS), f32),
            pltpu.VMEM((NZ, 16, HS), f32), pltpu.VMEM((NZ, 16, HS), f32),
            pltpu.VMEM((GROUP, 16, HS), f32), pltpu.VMEM((GROUP, 16, HS), f32),
            dma((n_head,)), dma((n_head,)),
            dma((GROUP,)), dma((GROUP,)), dma((GROUP,)), dma((GROUP,)),
            dma((NZ,)), dma((NZ,)), dma((NZ,)), dma((NZ,)),
            dma((GROUP,)), dma((GROUP,)), dma((GROUP,)), dma((GROUP,)),
        ],
        compiler_params=pltpu.CompilerParams(collective_id=1, has_side_effects=True, vmem_limit_bytes=12 << 20),
        name="reduce",
    )(acc, m_o, starts, kall, vall, q_s, t_s, g_s, low_t, b, tb, x)


def finish_kernel(a_ref, b_ref, oa_ref, ob_ref, sem):
    copies = [pltpu.make_async_copy(a_ref, oa_ref, sem.at[0]), pltpu.make_async_copy(b_ref, ob_ref, sem.at[1])]
    for c in copies:
        c.start()
    for c in copies:
        c.wait()


def finish(a, b):
    vm = pl.BlockSpec(memory_space=pltpu.VMEM)
    hb = pl.BlockSpec(memory_space=pltpu.HBM)
    return pl.pallas_call(
        finish_kernel,
        out_shape=(jax.ShapeDtypeStruct(a.shape, f32), jax.ShapeDtypeStruct(b.shape, f32)),
        in_specs=[vm, vm],
        out_specs=(hb, hb),
        scratch_shapes=[pltpu.SemaphoreType.DMA((2,))],
        compiler_params=pltpu.CompilerParams(vmem_limit_bytes=1 << 20),
        name="finish",
    )(a, b)


def on_device(n_ctx, n_head, activations, query_base, key_rows, values, out_cotangent, adapter_a, adapter_b, tangent_a, tangent_b,
              segment_ids, doc_starts):
    rows = activations.shape[0]
    kall, vall, low_t, x, b, tb, starts, q_s, t_s, g_s, acc, m_o = gather(
        key_rows, values, activations, adapter_a.T, tangent_a.T, query_base, out_cotangent, adapter_b, tangent_b,
        segment_ids, doc_starts, n_ctx, n_head)
    m_o, acc = attend(starts, m_o, q_s, t_s, g_s, kall, vall, acc, lambda: jnp.maximum(lax.axis_index("ctx") // GROUP - 1, 0), GROUP * rows)
    oa, ob = finish(*reduce(acc, m_o, starts, kall, vall, q_s, t_s, g_s, low_t, b, tb, x, n_head))
    return oa.T, ob


def solution(mesh):
    wide = P("ctx", "head")
    placed = (wide,) * 5 + (P("head", None), P(None, "head"), P("head", None), P(None, "head"), P("ctx"), P())
    return jax.shard_map(
        functools.partial(on_device, mesh.shape["ctx"], mesh.shape["head"]),
        mesh=mesh,
        in_specs=placed,
        out_specs=(P("head", None), P(None, "head")),
        check_vma=False,
    )
```
